128 devices in a mesh: dp: 8 (over y, core), expert: 16 (over z, x).
Axes of the slice: x: 4, y: 4, z: 4, core: 2. Of those that a mesh axis runs over, the one named last changes fastest.
Arguments:
- tokens: bfloat16 [24576, 4096], P(('dp', 'expert')), may hold values from -6 to 6
- cotangent: bfloat16 [24576, 4096], P(('dp', 'expert')), may hold values from -6 to 6
- expert_ids: int32 [24576, 6], P(('dp', 'expert')), may hold values from 0 to 63, as said below
- route_weights: float32 [24576, 6], P(('dp', 'expert')), may hold values from 0.05 to 1
- expert_weights: bfloat16 [16, 704, 3, 4096], P('expert'), may hold values from -0.09375 to 0.09375
Outputs:
- input_grad: bfloat16 [24576, 4096], P(('dp', 'expert'))
- route_grad: bfloat16 [24576, 6], P(('dp', 'expert'))
- weight_grad: float32 [16, 704, 3, 4096], P('expert', 'dp')
The draws below stay inside these ranges and needn't reach their ends.
Inputs may be any that keep to these rules, and one draw needn't show every extreme that they name: `expert_ids`: each row names 6 different experts. Only experts below 16 are in this window; in the rows of one device (aligned blocks of 192 rows) each of them is named at most 36 times.
All inputs are finite; a program needn't handle non-finite values.
Results may differ from the reference program's by a relative error of at most 0.015.
Values may be sent and summed in bfloat16 or wider, within the bound.
No kernel may reach another device: no remote copies, remote signals or barrier semaphores. Data moves between devices by JAX's collectives and lax.ppermute only.
A program may use at most 128 MiB of HBM per device.

```python
import math
import jax
import jax.numpy as jnp
from jax import lax

D = 4096
HID = 704
EXPERTS = 64
TOP = 6
TOK_DEV = 192
FLIGHT = 16
CAP = 36
TOKENS = 24576
N_DP = 8
N_EXPERT = 16


def draw_expert_ids(key, part):
    base_key = jax.random.fold_in(key, 11)
    block_total = TOKENS // TOK_DEV
    hottest = jax.random.randint(jax.random.fold_in(base_key, 7), (), 0, FLIGHT)
    others = EXPERTS - FLIGHT

    def one_block(block_key):
        load_key, order_key, turn_key = jax.random.split(block_key, 3)
        loads = jax.random.randint(load_key, (FLIGHT,), 0, CAP + 1)
        loads = jnp.where(jnp.arange(FLIGHT) == hottest, CAP, loads)
        remain = TOK_DEV * TOP - jnp.sum(loads)
        spare_index = jnp.arange(others)
        spare_loads = remain // others + (spare_index < remain % others).astype(jnp.int32)
        counts = jnp.concatenate([loads, spare_loads]).astype(jnp.int32)
        deck = jnp.repeat(jnp.arange(EXPERTS, dtype=jnp.int32), counts, total_repeat_length=TOK_DEV * TOP)
        dealt = deck.reshape(TOP, TOK_DEV).T
        order = jax.random.permutation(order_key, TOK_DEV)
        dealt = dealt[order]
        turns = jax.random.randint(turn_key, (TOK_DEV, 1), 0, TOP)
        columns = (jnp.arange(TOP)[None, :] + turns) % TOP
        return jnp.take_along_axis(dealt, columns, axis=1)
    block_keys = jax.random.split(base_key, block_total)
    return jax.vmap(one_block)(block_keys).reshape(TOKENS, TOP).astype(jnp.int32)


def block_levels(key, dims, shards, low, largest):
    loudness, own = 1.0, jax.random.fold_in(key, 6)
    for axis_at, blocks in shards:
        heights = jnp.exp(jax.random.uniform(jax.random.fold_in(own, axis_at), (blocks,), jnp.float32, low / len(shards), largest / len(shards)))
        loudness = loudness * jnp.repeat(heights, dims[axis_at] // blocks).reshape([-1 if axis == axis_at else 1 for axis in range(len(dims))])
    return loudness


def normal_values(key, extent, width, limit, shards=(), kind=jnp.bfloat16):
    drawn = width * jax.random.normal(key, extent, jnp.float32)
    if shards:
        drawn = drawn * block_levels(key, extent, shards, -0.22, 0.18)
    return jnp.clip(drawn, -limit, limit).astype(kind)


def setup_inputs(seed: int = 0) -> dict:
    key_list = jax.random.split(jax.random.key(seed), 6)
    return {
        "tokens": normal_values(key_list[0], (TOKENS, D), 1.0, 6.0, ((0, 128),)),
        "cotangent": normal_values(key_list[1], (TOKENS, D), 1.0, 6.0, ((0, 128),)),
        "expert_ids": draw_expert_ids(jax.random.fold_in(key_list[5], 71), 0),
        "route_weights": jnp.clip(jnp.exp(math.log(1.0) - 2.9957323 * jax.random.uniform(key_list[3], (TOKENS, TOP), jnp.float32) ** block_levels(key_list[3], (TOKENS, TOP), ((0, 128),), -0.2, 0.2)), 0.05, 1.0),
        "expert_weights": normal_values(key_list[4], (FLIGHT, HID, 3, D), D ** -0.5, 0.09375, ((0, 16),)),
    }


def expert_pass(token_rows, cot_rows, row_scale, weights):
    weights32 = weights.astype(jnp.float32)
    token32 = token_rows.astype(jnp.float32)
    cot32 = cot_rows.astype(jnp.float32)
    gate_pre = jnp.einsum("md,hd->mh", token32, weights32[:, 0, :])
    up_pre = jnp.einsum("md,hd->mh", token32, weights32[:, 1, :])
    logistic = jax.nn.sigmoid(gate_pre)
    hidden = (gate_pre * logistic * up_pre).astype(jnp.bfloat16)
    back_proj = jnp.einsum("md,hd->mh", cot32, weights32[:, 2, :])
    route_rows = jnp.sum(hidden.astype(jnp.float32) * back_proj, axis=1).astype(jnp.bfloat16)
    scale32 = row_scale.astype(jnp.float32)[:, None]
    scaled = (scale32 * cot32).astype(jnp.bfloat16)
    grad_hidden = scale32 * back_proj
    gate_delta = (grad_hidden * up_pre * logistic * (1.0 + gate_pre * (1.0 - logistic))).astype(jnp.bfloat16)
    up_delta = (grad_hidden * gate_pre * logistic).astype(jnp.bfloat16)
    gd32 = gate_delta.astype(jnp.float32)
    ud32 = up_delta.astype(jnp.float32)
    input_rows = (jnp.einsum("mh,hd->md", gd32, weights32[:, 0, :]) + jnp.einsum("mh,hd->md", ud32, weights32[:, 1, :])).astype(jnp.bfloat16)
    gate_term = jnp.einsum("mh,md->hd", gd32, token32)
    up_term = jnp.einsum("mh,md->hd", ud32, token32)
    down_term = jnp.einsum("mh,md->hd", hidden.astype(jnp.float32), scaled.astype(jnp.float32))
    term = jnp.stack([gate_term, up_term, down_term], axis=1)
    return input_rows, route_rows, term


def reference(tokens, cotangent, expert_ids, route_weights, expert_weights):
    group_rows = TOK_DEV * N_EXPERT
    route_count = group_rows * TOP
    slot_count = N_EXPERT * CAP

    def per_group(weight_acc, group_index):
        first_row = (group_index * group_rows).astype(jnp.int32)
        group_tokens = lax.dynamic_slice_in_dim(tokens, first_row, group_rows, 0)
        group_cot = lax.dynamic_slice_in_dim(cotangent, first_row, group_rows, 0)
        group_ids = lax.dynamic_slice_in_dim(expert_ids, first_row, group_rows, 0).reshape(-1)
        group_scale = lax.dynamic_slice_in_dim(route_weights, first_row, group_rows, 0).reshape(-1)

        def per_expert(carry, expert_index):
            input_acc, route_acc, weight_now = carry
            chosen = jnp.nonzero(group_ids == expert_index, size=slot_count, fill_value=route_count)[0].astype(jnp.int32)
            filled = chosen < route_count
            safe_index = jnp.minimum(chosen, route_count - 1)
            owner_row = safe_index // TOP
            zero16 = jnp.zeros((), jnp.bfloat16)
            token_rows = jnp.where(filled[:, None], group_tokens[owner_row], zero16)
            cot_rows = jnp.where(filled[:, None], group_cot[owner_row], zero16)
            row_scale = jnp.where(filled, group_scale[safe_index], jnp.float32(0.0)).astype(jnp.bfloat16)
            weights = lax.dynamic_index_in_dim(expert_weights, expert_index, 0, keepdims=False)
            input_rows, route_rows, term = expert_pass(token_rows, cot_rows, row_scale, weights)
            rounded = lax.optimization_barrier(term.astype(jnp.bfloat16)).astype(jnp.float32)
            weight_now = weight_now.at[expert_index].add(rounded)
            input_acc = input_acc.at[owner_row].add(jnp.where(filled[:, None], input_rows.astype(jnp.float32), jnp.float32(0.0)))
            route_acc = route_acc.at[safe_index].add(jnp.where(filled, route_rows.astype(jnp.float32), jnp.float32(0.0)))
            return (input_acc, route_acc, weight_now), None

        start = (jnp.zeros((group_rows, D), jnp.float32), jnp.zeros((route_count,), jnp.float32), weight_acc)
        finish, _ = lax.scan(per_expert, start, jnp.arange(FLIGHT, dtype=jnp.int32))
        input_acc, route_acc, weight_acc = finish
        return weight_acc, (input_acc.astype(jnp.bfloat16), route_acc.astype(jnp.bfloat16).reshape(group_rows, TOP))

    weight_start = jnp.zeros((FLIGHT, HID, 3, D), jnp.float32)
    weight_grad, outputs = lax.scan(per_group, weight_start, jnp.arange(N_DP, dtype=jnp.int32))
    input_grad = outputs[0].reshape(TOKENS, D)
    route_grad = outputs[1].reshape(TOKENS, TOP)
    return input_grad, route_grad, weight_grad
```

```python
import jax
import jax.numpy as jnp
from jax import lax
from jax.sharding import PartitionSpec as P

CAP = 36
SIDE = 4
BLOCK = SIDE * CAP
ROWS = SIDE * BLOCK
BACK = (0, 3, 2, 1)


def hop(dz, dx):
    return [
        (z * SIDE + x, (z + dz) % SIDE * SIDE + (x + dx) % SIDE)
        for z in range(SIDE)
        for x in range(SIDE)
    ]


def along(axis, step):
    return hop(step, 0) if axis == "z" else hop(0, step)


def move(value, axis, step):
    return lax.ppermute(value, "expert", along(axis, step)) if step % SIDE else value


def gather_ring(value, axis):
    half = value.shape[0] // 2
    from_before = move(value, axis, 1)
    from_after = move(value, axis, -1)
    far_low = move(from_before[:half], axis, 1)
    far_high = move(from_after[half:], axis, -1)
    return jnp.concatenate([value, from_after, far_low, far_high, from_before], axis=0)


def rolled(value, shift, axis):
    twice = jnp.concatenate([value, value], axis=axis)
    return lax.dynamic_slice_in_dim(twice, shift, SIDE, axis)


def one_hot(codes, count):
    rows = lax.broadcasted_iota(jnp.int32, (count, codes.shape[-1]), 0)
    return (rows == codes[None, :]).astype(jnp.bfloat16)


def pick(left, right):
    return jnp.dot(left, right, preferred_element_type=jnp.float32).astype(jnp.bfloat16)


def swap_matrix():
    row = lax.broadcasted_iota(jnp.int32, (ROWS, ROWS), 0)
    col = lax.broadcasted_iota(jnp.int32, (ROWS, ROWS), 1)
    block, slot = row // CAP, row % CAP
    return (col == ((block % SIDE) * SIDE + block // SIDE) * CAP + slot).astype(jnp.bfloat16)


def shards(tokens, cotangent, expert_ids, route_weights, expert_weights):
    me = lax.axis_index("expert")
    z, x = me // SIDE, me % SIDE
    tok_rows, width = tokens.shape
    half = width // 2
    experts = SIDE * SIDE

    ids = expert_ids.T
    column = lax.broadcasted_iota(jnp.int32, (experts, 1, 1), 0)
    named = ids[None] == column
    routed = jnp.any(named, axis=1)
    scale = jnp.sum(jnp.where(named, route_weights.T[None], 0.0), axis=1)
    earlier = (
        lax.broadcasted_iota(jnp.int32, (tok_rows, tok_rows), 0)
        < lax.broadcasted_iota(jnp.int32, (tok_rows, tok_rows), 1)
    ).astype(jnp.bfloat16)
    slots = jnp.dot(routed.astype(jnp.bfloat16), earlier, preferred_element_type=jnp.float32)
    slots = jnp.where(routed, slots, -1024.0)
    table = lax.all_gather(jnp.stack([slots, scale]), "expert", axis=0, tiled=False)
    table = table.reshape(SIDE, SIDE, 2, SIDE, SIDE, tok_rows)

    tok_all = gather_ring(tokens, "z")
    cot_all = gather_ring(cotangent, "x")

    all_slots = table[:, :, 0]
    base = jnp.array([CAP * b for b in BACK], jnp.float32)
    tok_code = lax.dynamic_index_in_dim(all_slots, x, 1, keepdims=False)
    tok_code = lax.dynamic_index_in_dim(tok_code, z, 1, keepdims=False)
    tok_code = rolled(rolled(tok_code, z, 0), x, 1) + base[:, None, None]
    tok_code = tok_code.transpose(1, 0, 2).reshape(SIDE, SIDE * tok_rows).astype(jnp.int32)
    cot_code = lax.dynamic_index_in_dim(all_slots, z, 0, keepdims=False)
    cot_code = lax.dynamic_index_in_dim(cot_code, x, 2, keepdims=False)
    cot_code = rolled(rolled(cot_code, x, 0), z, 1) + base[:, None, None]
    cot_code = cot_code.transpose(1, 0, 2).reshape(SIDE, SIDE * tok_rows).astype(jnp.int32)

    tok_parts = [None] * SIDE
    cot_parts = [None] * SIDE
    for k in (1, 3, 2, 0):
        tok_parts[k] = move(pick(one_hot(tok_code[k], BLOCK), tok_all), "x", k)
        cot_parts[k] = move(pick(one_hot(cot_code[k], BLOCK), cot_all), "z", k)
    token_rows = jnp.concatenate(tok_parts, axis=0)
    swap = swap_matrix()
    cot_rows = pick(swap, jnp.concatenate(cot_parts, axis=0))

    mine = lax.dynamic_index_in_dim(table, z, 3, keepdims=False)
    mine = lax.dynamic_index_in_dim(mine, x, 3, keepdims=False)
    mine = rolled(rolled(mine, z, 0), x, 1)
    mine = jnp.stack([mine[b] for b in BACK])
    mine = jnp.stack([mine[:, a] for a in BACK])
    slot_here = jnp.arange(CAP, dtype=jnp.float32)[None, None, :, None]
    row_scale = jnp.sum(
        jnp.where(mine[:, :, 0, None, :] == slot_here, mine[:, :, 1, None, :], 0.0), axis=-1
    )
    row_scale = row_scale.reshape(ROWS, 1).astype(jnp.bfloat16).astype(jnp.float32)

    weights = expert_weights[0]
    gate_w, up_w, down_w = weights[:, 0, :], weights[:, 1, :], weights[:, 2, :]
    gate_pre = jnp.einsum("md,hd->mh", token_rows, gate_w, preferred_element_type=jnp.float32)
    up_pre = jnp.einsum("md,hd->mh", token_rows, up_w, preferred_element_type=jnp.float32)
    back_proj = jnp.einsum("md,hd->mh", cot_rows, down_w, preferred_element_type=jnp.float32)
    logistic = jax.nn.sigmoid(gate_pre)
    hidden = (gate_pre * logistic * up_pre).astype(jnp.bfloat16)
    route_rows = jnp.sum(hidden.astype(jnp.float32) * back_proj, axis=1).astype(jnp.bfloat16)
    scaled = (row_scale * cot_rows.astype(jnp.float32)).astype(jnp.bfloat16)
    grad_hidden = row_scale * back_proj
    gate_delta = (grad_hidden * up_pre * logistic * (1.0 + gate_pre * (1.0 - logistic))).astype(
        jnp.bfloat16
    )
    up_delta = (grad_hidden * gate_pre * logistic).astype(jnp.bfloat16)

    route_all = lax.all_gather(
        route_rows.astype(jnp.float32).reshape(8, -1), "expert", axis=0, tiled=False
    )

    terms = [
        jnp.einsum("mh,md->hd", left, right, preferred_element_type=jnp.float32)
        .astype(jnp.bfloat16)
        .reshape(8, -1, width)
        for left, right in (
            (gate_delta, token_rows),
            (up_delta, token_rows),
            (hidden, scaled),
        )
    ]
    summed = lax.psum_scatter(
        jnp.stack(terms, axis=1), "dp", scatter_dimension=0, tiled=True
    ).astype(jnp.float32)
    weight_grad = summed.transpose(0, 2, 1, 3)

    deltas = jnp.concatenate([gate_delta, up_delta], axis=1)
    deltas_swapped = pick(swap, deltas)

    def inputs(rows, columns):
        both = jnp.concatenate([gate_w[:, columns], up_w[:, columns]], axis=0)
        return pick(rows, both)

    def back(rows, first, second):
        got = [move(rows[p * BLOCK : (p + 1) * BLOCK], first, -p) for p in range(SIDE)]
        turned = pick(swap, jnp.concatenate(got, axis=0))
        got = [move(turned[p * BLOCK : (p + 1) * BLOCK], second, -p) for p in range(SIDE)]
        return jnp.concatenate(got, axis=0)

    left_rows = back(inputs(deltas, slice(0, half)), "x", "z")
    right_rows = back(inputs(deltas_swapped, slice(half, width)), "z", "x")

    expert = lax.broadcasted_iota(jnp.int32, (experts, 1), 0)
    near_z, near_x = (expert // SIDE - z) % SIDE, (expert % SIDE - x) % SIDE
    own_slots = slots.astype(jnp.int32)
    route_named = named.astype(jnp.int32)

    def combine(rows, blocks):
        code = own_slots + blocks * CAP
        code = jnp.sum(route_named * code[:, None, :], axis=0)
        live = jnp.any(named, axis=0)
        code = jnp.where(live, code, -1)
        hit = lax.broadcasted_iota(jnp.int32, (ROWS, tok_rows), 0)
        hot = (hit == code[0][None, :])
        for k in range(1, code.shape[0]):
            hot = hot | (hit == code[k][None, :])
        return jnp.einsum(
            "ct,cd->td", hot.astype(jnp.bfloat16), rows, preferred_element_type=jnp.float32
        ).astype(jnp.bfloat16)

    input_grad = jnp.concatenate(
        [
            combine(left_rows, near_z * SIDE + near_x),
            combine(right_rows, near_x * SIDE + near_z),
        ],
        axis=1,
    )

    route_all = route_all.reshape(experts, experts, CAP).astype(jnp.float32)
    place = (near_x * SIDE + near_z) == lax.broadcasted_iota(jnp.int32, (experts, experts), 1)
    route_mine = jnp.sum(jnp.where(place[:, :, None], route_all, 0.0), axis=1)
    at_slot = slots[:, None, :] == jnp.arange(CAP, dtype=jnp.float32)[None, :, None]
    by_expert = jnp.sum(jnp.where(at_slot, route_mine[:, :, None], 0.0), axis=1)
    route_grad = jnp.sum(jnp.where(named, by_expert[:, None, :], 0.0), axis=0)
    return input_grad, route_grad.astype(jnp.bfloat16).T, weight_grad


def solution(mesh):
    rows = P(("dp", "expert"), None)
    return jax.shard_map(
        shards,
        mesh=mesh,
        in_specs=(rows, rows, rows, rows, P("expert", None, None, None)),
        out_specs=(rows, rows, P("expert", "dp", None, None)),
        check_vma=False,
    )
```

```python
import functools

import jax
import jax.numpy as jnp
from jax import lax
from jax.experimental import pallas as pl
from jax.experimental.pallas import tpu as pltpu
from jax.sharding import PartitionSpec as P

CAP = 36
SIDE = 4
BLOCK = SIDE * CAP
ROWS = SIDE * BLOCK
EXTRA = 128
HOPS = (0, 1, 3, 2)
PLACE = (0, 1, 3, 2)
BIG = 56 << 20


def hop(dz, dx):
    return [
        (z * SIDE + x, (z + dz) % SIDE * SIDE + (x + dx) % SIDE)
        for z in range(SIDE)
        for x in range(SIDE)
    ]


def move(value, axis, step):
    if step % SIDE == 0:
        return value
    return lax.ppermute(value, "expert", hop(step, 0) if axis == "z" else hop(0, step))


def spread(blocks, axis, sign):
    return [move(blocks[p], axis, sign * HOPS[p]) for p in range(SIDE)]


def product(left, right, dims=((1,), (0,))):
    return lax.dot_general(left, right, (dims, ((), ())), preferred_element_type=jnp.float32)


def swap_matrix():
    row = jnp.arange(ROWS, dtype=jnp.int32)[:, None]
    col = jnp.arange(ROWS, dtype=jnp.int32)[None, :]
    block, slot = row // CAP, row % CAP
    return (col == ((block % SIDE) * SIDE + block // SIDE) * CAP + slot).astype(jnp.bfloat16)


def params(*axes):
    return pltpu.CompilerParams(dimension_semantics=axes, vmem_limit_bytes=BIG)


def cost(flops, moved):
    return pl.CostEstimate(flops=int(flops), bytes_accessed=int(moved), transcendentals=0)


def swap_kernel(matrix_ref, *refs):
    rows = jnp.concatenate([ref[...] for ref in refs[:SIDE]], axis=0)
    out = product(matrix_ref[...], rows).astype(jnp.bfloat16)
    for p in range(SIDE):
        refs[SIDE + p][...] = out[p * BLOCK : (p + 1) * BLOCK]


def swap_blocks(matrix, blocks):
    width = blocks[0].shape[1]
    tile = 1024 if width % 1024 == 0 else 1408 if width % 1408 == 0 else width
    spec = pl.BlockSpec((BLOCK, tile), lambda i: (0, i))
    return pl.pallas_call(
        swap_kernel,
        grid=(width // tile,),
        in_specs=[pl.BlockSpec((ROWS, ROWS), lambda i: (0, 0))] + [spec] * SIDE,
        out_specs=[spec] * SIDE,
        out_shape=[jax.ShapeDtypeStruct((BLOCK, width), jnp.bfloat16)] * SIDE,
        compiler_params=params("arbitrary"),
        cost_estimate=cost(2 * ROWS * ROWS * width, 4 * ROWS * width),
        name="swap_blocks",
    )(matrix, *blocks)


def forward_kernel(steps, matrix_ref, weight_ref, *refs):
    toks, cots, scales = refs[0:4], refs[4:8], refs[8:12]
    gate_out, up_out, hidden_out, gate_turned, up_turned, route_out = refs[12:18]
    gate_acc, up_acc, back_acc = refs[18:21]
    step = pl.program_id(0)

    @pl.when(step == 0)
    def _():
        gate_acc[...] = jnp.zeros_like(gate_acc)
        up_acc[...] = jnp.zeros_like(up_acc)
        back_acc[...] = jnp.zeros_like(back_acc)

    tok = jnp.concatenate([ref[...] for ref in toks], axis=0)
    cot = jnp.concatenate([ref[...] for ref in cots], axis=0)
    last = ((1,), (1,))
    gate_acc[...] += product(tok, weight_ref[0], last)
    up_acc[...] += product(tok, weight_ref[1], last)
    back_acc[...] += product(cot, weight_ref[2], last)

    @pl.when(step == steps - 1)
    def _():
        matrix = matrix_ref[...]
        gate_pre, up_pre, back = gate_acc[...], up_acc[...], back_acc[...]
        scale = jnp.concatenate([ref[:, :1] for ref in scales], axis=0).astype(jnp.float32)
        logistic = 1.0 / (1.0 + jnp.exp(-gate_pre))
        gated = gate_pre * logistic
        hidden = (gated * up_pre).astype(jnp.bfloat16)
        hidden_turned = product(matrix, hidden)
        hidden_out[...] = hidden_turned.astype(jnp.bfloat16)
        route = jnp.sum(hidden_turned * back, axis=1, keepdims=True).astype(jnp.bfloat16)
        route = jnp.broadcast_to(route, (ROWS, EXTRA))
        route_out[...] = product(matrix, route).astype(jnp.bfloat16)
        grad = scale * back
        high = grad.astype(jnp.bfloat16)
        low = (grad - high.astype(jnp.float32)).astype(jnp.bfloat16)
        grad = product(matrix, high) + product(matrix, low)
        gate_delta = (grad * up_pre * logistic * (1.0 + gate_pre * (1.0 - logistic))).astype(
            jnp.bfloat16
        )
        up_delta = (grad * gated).astype(jnp.bfloat16)
        gate_out[...] = gate_delta
        up_out[...] = up_delta
        gate_turned[...] = product(matrix, gate_delta).astype(jnp.bfloat16)
        up_turned[...] = product(matrix, up_delta).astype(jnp.bfloat16)


def forward(matrix, weights, toks, cots):
    units, width = weights.shape[1:]
    tile = 512
    steps = width // tile
    rows = pl.BlockSpec((BLOCK, tile), lambda i: (0, i))
    extra = pl.BlockSpec((BLOCK, EXTRA), lambda i: (0, width // EXTRA))
    whole = pl.BlockSpec((ROWS, units), lambda i: (0, 0))
    small = jax.ShapeDtypeStruct((ROWS, units), jnp.bfloat16)
    return pl.pallas_call(
        functools.partial(forward_kernel, steps),
        grid=(steps,),
        in_specs=[
            pl.BlockSpec((ROWS, ROWS), lambda i: (0, 0)),
            pl.BlockSpec((3, units, tile), lambda i: (0, 0, i)),
        ]
        + [rows] * 8
        + [extra] * 4,
        out_specs=[whole] * 5 + [pl.BlockSpec((ROWS, EXTRA), lambda i: (0, 0))],
        out_shape=[small] * 5 + [jax.ShapeDtypeStruct((ROWS, EXTRA), jnp.bfloat16)],
        scratch_shapes=[pltpu.VMEM((ROWS, units), jnp.float32)] * 3,
        compiler_params=params("arbitrary"),
        cost_estimate=cost(6 * ROWS * units * width, 6 * units * width + 4 * ROWS * width),
        name="forward",
    )(matrix, weights, *toks, *cots, *cots)


def terms_kernel(gate_ref, up_ref, hidden_ref, *refs):
    toks, cots, scales, out_ref = refs[0:4], refs[4:8], refs[8:12], refs[12]
    tok = jnp.concatenate([ref[...] for ref in toks], axis=0)
    scaled = jnp.concatenate(
        [
            (ref[...].astype(jnp.float32) * scale[:, :1].astype(jnp.float32)).astype(jnp.bfloat16)
            for ref, scale in zip(cots, scales)
        ],
        axis=0,
    )
    share = out_ref.shape[2]
    for kind, (left, right) in enumerate(
        ((gate_ref, tok), (up_ref, tok), (hidden_ref, scaled))
    ):
        term = product(left[...], right, ((0,), (0,))).astype(jnp.bfloat16)
        for owner in range(out_ref.shape[0]):
            out_ref[owner, kind] = term[owner * share : (owner + 1) * share]


def terms(gate_delta, up_delta, hidden, toks, cots, owners):
    units = gate_delta.shape[1]
    width = toks[0].shape[1]
    tile = 512
    rows = pl.BlockSpec((BLOCK, tile), lambda i: (0, i))
    extra = pl.BlockSpec((BLOCK, EXTRA), lambda i: (0, width // EXTRA))
    whole = pl.BlockSpec((ROWS, units), lambda i: (0, 0))
    share = units // owners
    return pl.pallas_call(
        terms_kernel,
        grid=(width // tile,),
        in_specs=[whole] * 3 + [rows] * 8 + [extra] * 4,
        out_specs=pl.BlockSpec((owners, 3, share, tile), lambda i: (0, 0, 0, i)),
        out_shape=jax.ShapeDtypeStruct((owners, 3, share, width), jnp.bfloat16),
        compiler_params=params("arbitrary"),
        cost_estimate=cost(6 * ROWS * units * width, 6 * units * width + 4 * ROWS * width),
        name="terms",
    )(gate_delta, up_delta, hidden, *toks, *cots, *cots)


def inputs_kernel(tiles, gate_ref, up_ref, weight_ref, *refs):
    def columns():
        return (product(gate_ref[...], weight_ref[0]) + product(up_ref[...], weight_ref[1])).astype(
            jnp.bfloat16
        )

    def put(value, width):
        for p in range(SIDE):
            refs[-SIDE + p][:, :width] = value[p * BLOCK : (p + 1) * BLOCK]

    put(columns(), weight_ref.shape[2])


def inputs(gate_delta, up_delta, weights, first, count):
    units = weights.shape[1]
    tile = 512
    whole = pl.BlockSpec((ROWS, units), lambda i: (0, 0))
    return pl.pallas_call(
        functools.partial(inputs_kernel, count // tile),
        grid=(count // tile,),
        in_specs=[
            whole,
            whole,
            pl.BlockSpec((2, units, tile), lambda i: (0, 0, first // tile + i)),
        ],
        out_specs=[pl.BlockSpec((BLOCK, tile), lambda i: (0, i))] * SIDE,
        out_shape=[jax.ShapeDtypeStruct((BLOCK, count), jnp.bfloat16)] * SIDE,
        compiler_params=params("arbitrary"),
        cost_estimate=cost(4 * ROWS * units * count, 4 * units * count + 2 * ROWS * count),
        name="inputs",
    )(gate_delta, up_delta, weights)


def shards(tokens, cotangent, expert_ids, route_weights, expert_weights):
    me = lax.axis_index("expert")
    z, x = me // SIDE, me % SIDE
    tok_rows, width = tokens.shape
    half = width // 2
    experts = SIDE * SIDE
    owners = lax.axis_size("dp")

    ids = expert_ids.T
    column = lax.broadcasted_iota(jnp.int32, (experts, 1, 1), 0)
    named = ids[None] == column
    routed = jnp.any(named, axis=1)
    earlier = (
        lax.broadcasted_iota(jnp.int32, (tok_rows, tok_rows), 0)
        < lax.broadcasted_iota(jnp.int32, (tok_rows, tok_rows), 1)
    ).astype(jnp.bfloat16)
    slots = jnp.dot(routed.astype(jnp.bfloat16), earlier, preferred_element_type=jnp.float32)
    slots = slots.astype(jnp.int32)
    expert = lax.broadcasted_iota(jnp.int32, (experts, 1), 0)
    far_z, far_x = (expert // SIDE - z) % SIDE, (expert % SIDE - x) % SIDE
    near_z = jnp.where(far_z >= 2, 5 - far_z, far_z)
    near_x = jnp.where(far_x >= 2, 5 - far_x, far_x)
    live = jnp.any(named, axis=0)

    def codes(blocks):
        code = jnp.sum(jnp.where(named, (slots + blocks * CAP)[:, None, :], 0), axis=0)
        return jnp.where(live, code, -1)

    def one_hot(code, first, count):
        row = lax.broadcasted_iota(jnp.int32, (count, tok_rows), 0) + first
        hot = row == code[0][None, :]
        for k in range(1, code.shape[0]):
            hot = hot | (row == code[k][None, :])
        return hot.astype(jnp.bfloat16)

    z_first = codes(near_z * SIDE + near_x)
    x_first = codes(near_x * SIDE + near_z)

    def row_scales(code, first):
        row = lax.broadcasted_iota(jnp.int32, (BLOCK, 1, 1), 0) + first
        scale = jnp.where(row == code[None], route_weights.T[None], 0.0)
        return jnp.sum(scale, axis=(1, 2))[:, None].astype(jnp.bfloat16)

    def pick(left, right):
        return jnp.dot(left, right, preferred_element_type=jnp.float32).astype(jnp.bfloat16)

    tok_blocks, cot_blocks = [], []
    for p in range(SIDE):
        tok_blocks.append(pick(one_hot(z_first, p * BLOCK, BLOCK), tokens))
        picked = pick(one_hot(x_first, p * BLOCK, BLOCK), cotangent)
        scale = jnp.broadcast_to(row_scales(x_first, p * BLOCK), (BLOCK, EXTRA))
        cot_blocks.append(jnp.concatenate([picked, scale], axis=1))

    matrix = swap_matrix()
    toks = spread(swap_blocks(matrix, spread(tok_blocks, "z", 1)), "x", 1)
    cots = spread(swap_blocks(matrix, spread(cot_blocks, "x", 1)), "z", 1)

    weights = expert_weights[0].transpose(1, 0, 2)
    gate_delta, up_delta, hidden, gate_turned, up_turned, route = forward(
        matrix, weights, toks, cots
    )
    partial_sums = terms(gate_delta, up_delta, hidden, toks, cots, owners)
    summed = lax.psum_scatter(partial_sums, "dp", scatter_dimension=0, tiled=True)
    weight_grad = summed.astype(jnp.float32).transpose(0, 2, 1, 3)

    left = inputs(gate_delta, up_delta, weights, 0, half)
    right = inputs(gate_turned, up_turned, weights, half, half)
    left = [
        jnp.concatenate([left[p], route[p * BLOCK : (p + 1) * BLOCK]], axis=1)
        for p in range(SIDE)
    ]
    left = spread(swap_blocks(matrix, spread(left, "x", -1)), "z", -1)
    right = spread(swap_blocks(matrix, spread(right, "z", -1)), "x", -1)

    def combine(blocks, code):
        return jnp.einsum(
            "ct,cd->td",
            one_hot(code, 0, ROWS),
            jnp.concatenate(blocks, axis=0),
            preferred_element_type=jnp.float32,
        ).astype(jnp.bfloat16)

    input_grad = jnp.concatenate(
        [combine([b[:, :half] for b in left], z_first), combine(right, x_first)], axis=1
    )
    route_mine = jnp.concatenate([b[:, half] for b in left], axis=0).astype(jnp.float32)
    row = lax.broadcasted_iota(jnp.int32, (ROWS, 1, 1), 0)
    route_grad = jnp.sum(jnp.where(row == z_first[None], route_mine[:, None, None], 0.0), axis=0)
    return input_grad, route_grad.astype(jnp.bfloat16).T, weight_grad


def solution(mesh):
    rows = P(("dp", "expert"), None)
    return jax.shard_map(
        shards,
        mesh=mesh,
        in_specs=(rows, rows, rows, rows, P("expert", None, None, None)),
        out_specs=(rows, rows, P("expert", "dp", None, None)),
        check_vma=False,
    )
```

```python
import functools

import jax
import jax.numpy as jnp
from jax import lax
from jax.experimental import pallas as pl
from jax.experimental.pallas import tpu as pltpu
from jax.sharding import PartitionSpec as P

CAP = 36
SIDE = 4
BLOCK = SIDE * CAP
ROWS = SIDE * BLOCK
EXTRA = 128
HOPS = (0, 1, 3, 2)
MAIN = 32
TAIL = CAP - MAIN
EARLY = 384
BIG = 56 << 20


def hop(dz, dx):
    return [
        (z * SIDE + x, (z + dz) % SIDE * SIDE + (x + dx) % SIDE)
        for z in range(SIDE)
        for x in range(SIDE)
    ]


def move(value, axis, step):
    if step % SIDE == 0:
        return value
    return lax.ppermute(value, "expert", hop(step, 0) if axis == "z" else hop(0, step))


def spread(blocks, axis, sign):
    return [move(blocks[p], axis, sign * HOPS[p]) for p in range(SIDE)]


def product(left, right, dims=((1,), (0,))):
    return lax.dot_general(left, right, (dims, ((), ())), preferred_element_type=jnp.float32)


def place(block, lane, slot):
    inner = jnp.where(slot < MAIN, lane * MAIN + slot, SIDE * MAIN + lane * TAIL + slot - MAIN)
    return block * BLOCK + inner


def swap_matrix(tails):
    size = SIDE * SIDE * TAIL if tails else ROWS
    row = jnp.arange(size, dtype=jnp.int32)
    if tails:
        source = row // TAIL % SIDE * SIDE * TAIL + row // TAIL // SIDE * TAIL + row % TAIL
    else:
        block, inner = row // BLOCK, row % BLOCK
        tail = inner - SIDE * MAIN
        lane = jnp.where(tail < 0, inner // MAIN, tail // TAIL)
        slot = jnp.where(tail < 0, inner % MAIN, MAIN + tail % TAIL)
        source = place(lane, block, slot)
    return (source[:, None] == row[None, :]).astype(jnp.bfloat16)


def params():
    return pltpu.CompilerParams(dimension_semantics=("arbitrary",), vmem_limit_bytes=BIG)


def cost(flops, moved):
    return pl.CostEstimate(flops=int(flops), bytes_accessed=int(moved), transcendentals=0)


def swap_kernel(matrix_ref, *refs):
    ins, outs = refs[:SIDE], refs[SIDE:]
    for p in range(SIDE):
        for q in range(SIDE):
            outs[q][p * MAIN : (p + 1) * MAIN] = ins[p][q * MAIN : (q + 1) * MAIN]
    tails = jnp.concatenate([ref[SIDE * MAIN :] for ref in ins], axis=0)
    tails = product(matrix_ref[...], tails).astype(jnp.bfloat16)
    for q in range(SIDE):
        outs[q][SIDE * MAIN :] = tails[q * SIDE * TAIL : (q + 1) * SIDE * TAIL]


def swap_blocks(matrix, blocks):
    width = blocks[0].shape[1]
    tile = 1024 if width % 1024 == 0 else 1408 if width % 1408 == 0 else width
    spec = pl.BlockSpec((BLOCK, tile), lambda i: (0, i))
    return pl.pallas_call(
        swap_kernel,
        grid=(width // tile,),
        in_specs=[pl.BlockSpec(matrix.shape, lambda i: (0, 0))] + [spec] * SIDE,
        out_specs=[spec] * SIDE,
        out_shape=[jax.ShapeDtypeStruct((BLOCK, width), jnp.bfloat16)] * SIDE,
        compiler_params=params(),
        cost_estimate=cost(2 * 64 * 64 * width, 4 * ROWS * width),
        name="swap_blocks",
    )(matrix, *blocks)


LAST = ((1,), (1,))


def early_kernel(weight_ref, *refs):
    toks, cots, outs = refs[0:3], refs[3:6], refs[6:9]

    @pl.when(pl.program_id(0) == 0)
    def _():
        for out in outs:
            out[...] = jnp.zeros_like(out)

    tok, cot = (
        jnp.concatenate([r[0][...], r[1][...], r[2][: EARLY - 2 * BLOCK]], axis=0)
        for r in (toks, cots)
    )
    for kind, right in enumerate((tok, tok, cot)):
        outs[kind][...] += product(weight_ref[kind], right, LAST)


def forward_early(weights, toks, cots):
    units, width = weights.shape[1:]
    tile = 1024
    rows = pl.BlockSpec((BLOCK, tile), lambda i: (0, i))
    whole = pl.BlockSpec((units, EARLY), lambda i: (0, 0))
    return pl.pallas_call(
        early_kernel,
        grid=(width // tile,),
        in_specs=[pl.BlockSpec((3, units, tile), lambda i: (0, 0, i))] + [rows] * 6,
        out_specs=[whole] * 3,
        out_shape=[jax.ShapeDtypeStruct((units, EARLY), jnp.float32)] * 3,
        compiler_params=params(),
        cost_estimate=cost(6 * EARLY * units * width, 6 * units * width + 4 * EARLY * width),
        name="forward_early",
    )(weights, *toks, *cots)


def late_kernel(steps, matrix_ref, weight_ref, *refs):
    toks, cots, scales = refs[0:2], refs[2:4], refs[4:8]
    early = refs[8:11]
    gate_out, up_out, hidden_out, route_out = refs[11:15]
    accs = refs[15:18]
    step = pl.program_id(0)

    @pl.when(step == 0)
    def _():
        for acc in accs:
            acc[...] = jnp.zeros_like(acc)

    tok, cot = (
        jnp.concatenate([r[0][EARLY - 2 * BLOCK :], r[1][...]], axis=0) for r in (toks, cots)
    )
    for kind, right in enumerate((tok, tok, cot)):
        accs[kind][...] += product(weight_ref[kind], right, LAST)

    @pl.when(step == steps - 1)
    def _():
        matrix = matrix_ref[...]
        gate_pre, up_pre, back = (
            jnp.concatenate([first[...], acc[...]], axis=1) for first, acc in zip(early, accs)
        )
        lane = lax.broadcasted_iota(jnp.int32, (8, EXTRA), 1)
        first_lane = jnp.where(lane == 0, 1.0, 0.0).astype(jnp.bfloat16)
        scale = jnp.concatenate([ref[...] for ref in scales], axis=0)
        scale = product(first_lane, scale, LAST)[:1]
        grad = scale * back
        high = grad.astype(jnp.bfloat16)
        low = (grad - high.astype(jnp.float32)).astype(jnp.bfloat16)
        grad = product(high, matrix) + product(low, matrix)
        logistic = 1.0 / (1.0 + jnp.exp(-gate_pre))
        gated = gate_pre * logistic
        hidden = product((gated * up_pre).astype(jnp.bfloat16), matrix)
        hidden_out[...] = hidden.astype(jnp.bfloat16)
        gate_out[...] = (grad * up_pre * logistic * (1.0 + gate_pre * (1.0 - logistic))).astype(
            jnp.bfloat16
        )
        up_out[...] = (grad * gated).astype(jnp.bfloat16)
        route = jnp.sum(hidden * back, axis=0, keepdims=True).astype(jnp.bfloat16)
        route_out[...] = product(matrix, jnp.broadcast_to(route, (EXTRA, ROWS)), LAST).astype(
            jnp.bfloat16
        )


def forward_late(matrix, weights, toks, cots, early):
    units, width = weights.shape[1:]
    tile = 1024
    steps = width // tile
    rows = pl.BlockSpec((BLOCK, tile), lambda i: (0, i))
    extra = pl.BlockSpec((BLOCK, EXTRA), lambda i: (0, width // EXTRA))
    whole = pl.BlockSpec((units, ROWS), lambda i: (0, 0))
    small = jax.ShapeDtypeStruct((units, ROWS), jnp.bfloat16)
    late = ROWS - EARLY
    return pl.pallas_call(
        functools.partial(late_kernel, steps),
        grid=(steps,),
        in_specs=[
            pl.BlockSpec((ROWS, ROWS), lambda i: (0, 0)),
            pl.BlockSpec((3, units, tile), lambda i: (0, 0, i)),
        ]
        + [rows] * 4
        + [extra] * 4
        + [pl.BlockSpec((units, EARLY), lambda i: (0, 0))] * 3,
        out_specs=[whole] * 3 + [pl.BlockSpec((ROWS, EXTRA), lambda i: (0, 0))],
        out_shape=[small] * 3 + [jax.ShapeDtypeStruct((ROWS, EXTRA), jnp.bfloat16)],
        scratch_shapes=[pltpu.VMEM((units, late), jnp.float32)] * 3,
        compiler_params=params(),
        cost_estimate=cost(6 * late * units * width, 6 * units * width + 12 * EARLY * units),
        name="forward_late",
    )(matrix, weights, *toks[2:], *cots[2:], *cots, *early)


def terms_kernel(gate_ref, up_ref, hidden_ref, *refs):
    toks, cots, scales, out_ref = refs[0:4], refs[4:8], refs[8:12], refs[12]
    tok = jnp.concatenate([ref[...] for ref in toks], axis=0)
    scaled = jnp.concatenate(
        [
            (ref[...].astype(jnp.float32) * scale[:, :1].astype(jnp.float32)).astype(jnp.bfloat16)
            for ref, scale in zip(cots, scales)
        ],
        axis=0,
    )
    share = out_ref.shape[2]
    for kind, (left, right) in enumerate(((gate_ref, tok), (up_ref, tok), (hidden_ref, scaled))):
        term = product(left[...], right)
        for owner in range(out_ref.shape[0]):
            out_ref[owner, kind] = term[owner * share : (owner + 1) * share].astype(jnp.bfloat16)


def terms(gate_delta, up_delta, hidden, toks, cots, owners):
    units = gate_delta.shape[0]
    width = toks[0].shape[1]
    tile = 512
    rows = pl.BlockSpec((BLOCK, tile), lambda i: (0, i))
    extra = pl.BlockSpec((BLOCK, EXTRA), lambda i: (0, width // EXTRA))
    whole = pl.BlockSpec((units, ROWS), lambda i: (0, 0))
    share = units // owners
    return pl.pallas_call(
        terms_kernel,
        grid=(width // tile,),
        in_specs=[whole] * 3 + [rows] * 8 + [extra] * 4,
        out_specs=pl.BlockSpec((owners, 3, share, tile), lambda i: (0, 0, 0, i)),
        out_shape=jax.ShapeDtypeStruct((owners, 3, share, width), jnp.bfloat16),
        compiler_params=params(),
        cost_estimate=cost(6 * ROWS * units * width, 6 * units * width + 4 * ROWS * width),
        name="terms",
    )(gate_delta, up_delta, hidden, *toks, *cots, *cots)


def inputs_kernel(tile, turn_ref, gate_ref, up_ref, weight_ref, route_ref, *refs):
    outs, (gate_rows, up_rows) = refs[:SIDE], refs[SIDE:]
    step = pl.program_id(0)

    @pl.when(step == 0)
    def _():
        gate_rows[...] = product(turn_ref[...], gate_ref[...], LAST).astype(jnp.bfloat16)
        up_rows[...] = product(turn_ref[...], up_ref[...], LAST).astype(jnp.bfloat16)
        for p in range(SIDE):
            width = outs[p].shape[1]
            if width % tile:
                outs[p][:, width - EXTRA :] = route_ref[p * BLOCK : (p + 1) * BLOCK]

    value = product(gate_rows[...], weight_ref[0]) + product(up_rows[...], weight_ref[1])
    value = value.astype(jnp.bfloat16)
    columns = pl.ds(pl.multiple_of(step * tile, tile), tile)
    for p in range(SIDE):
        outs[p][:, columns] = value[p * BLOCK : (p + 1) * BLOCK]


def inputs(turn, gate_delta, up_delta, weights, route, first, count, extra):
    units = weights.shape[1]
    tile = 512
    whole = pl.BlockSpec((units, ROWS), lambda i: (0, 0))
    block = (BLOCK, count + extra)
    return pl.pallas_call(
        functools.partial(inputs_kernel, tile),
        grid=(count // tile,),
        in_specs=[
            pl.BlockSpec((ROWS, ROWS), lambda i: (0, 0)),
            whole,
            whole,
            pl.BlockSpec((2, units, tile), lambda i: (0, 0, first // tile + i)),
            pl.BlockSpec((ROWS, EXTRA), lambda i: (0, 0)),
        ],
        out_specs=[pl.BlockSpec(block, lambda i: (0, 0))] * SIDE,
        out_shape=[jax.ShapeDtypeStruct(block, jnp.bfloat16)] * SIDE,
        scratch_shapes=[pltpu.VMEM((ROWS, units), jnp.bfloat16)] * 2,
        compiler_params=params(),
        cost_estimate=cost(4 * ROWS * units * count, 4 * units * count + 2 * ROWS * count),
        name="inputs",
    )(turn, gate_delta, up_delta, weights, route)


def shards(tokens, cotangent, expert_ids, route_weights, expert_weights):
    me = lax.axis_index("expert")
    z, x = me // SIDE, me % SIDE
    tok_rows, width = tokens.shape
    half = width // 2
    experts = SIDE * SIDE
    owners = lax.axis_size("dp")

    ids = expert_ids.T
    column = lax.broadcasted_iota(jnp.int32, (experts, 1, 1), 0)
    named = ids[None] == column
    routed = jnp.any(named, axis=1)
    earlier = (
        lax.broadcasted_iota(jnp.int32, (tok_rows, tok_rows), 0)
        < lax.broadcasted_iota(jnp.int32, (tok_rows, tok_rows), 1)
    ).astype(jnp.bfloat16)
    slots = jnp.dot(routed.astype(jnp.bfloat16), earlier, preferred_element_type=jnp.float32)
    slots = slots.astype(jnp.int32)
    expert = lax.broadcasted_iota(jnp.int32, (experts, 1), 0)
    far_z, far_x = (expert // SIDE - z) % SIDE, (expert % SIDE - x) % SIDE
    near_z = jnp.where(far_z >= 2, 5 - far_z, far_z)
    near_x = jnp.where(far_x >= 2, 5 - far_x, far_x)
    live = jnp.any(named, axis=0)

    def codes(block, lane):
        row = place(block, lane, slots)
        return jnp.where(live, jnp.sum(jnp.where(named, row[:, None, :], 0), axis=0), -1)

    def one_hot(code, first, count):
        row = lax.broadcasted_iota(jnp.int32, (count, tok_rows), 0) + first
        hot = row == code[0][None, :]
        for k in range(1, code.shape[0]):
            hot = hot | (row == code[k][None, :])
        return hot.astype(jnp.bfloat16)

    z_first = codes(near_z, near_x)
    x_first = codes(near_x, near_z)

    def row_scales(code, first):
        row = lax.broadcasted_iota(jnp.int32, (BLOCK, 1, 1), 0) + first
        scale = jnp.where(row == code[None], route_weights.T[None], 0.0)
        return jnp.sum(scale, axis=(1, 2))[:, None].astype(jnp.bfloat16)

    def pick(left, right):
        return jnp.dot(left, right, preferred_element_type=jnp.float32).astype(jnp.bfloat16)

    tok_blocks, cot_blocks = [], []
    for p in range(SIDE):
        tok_blocks.append(pick(one_hot(z_first, p * BLOCK, BLOCK), tokens))
        picked = pick(one_hot(x_first, p * BLOCK, BLOCK), cotangent)
        scale = jnp.broadcast_to(row_scales(x_first, p * BLOCK), (BLOCK, EXTRA))
        cot_blocks.append(jnp.concatenate([picked, scale], axis=1))

    turn = swap_matrix(False)
    small_turn = swap_matrix(True)
    same = (jnp.arange(ROWS)[:, None] == jnp.arange(ROWS)[None, :]).astype(jnp.bfloat16)

    def near_then_far(blocks, axis):
        near = [blocks[0]] + [move(blocks[p], axis, HOPS[p]) for p in (1, 2)]
        far = lax.optimization_barrier((blocks[3], near[1], near[2]))
        return [near[0], far[1], far[2], move(far[0], axis, HOPS[3])]

    toks = near_then_far(swap_blocks(small_turn, spread(tok_blocks, "z", 1)), "x")
    cots = near_then_far(swap_blocks(small_turn, spread(cot_blocks, "x", 1)), "z")

    weights = expert_weights[0].transpose(1, 0, 2)
    early = forward_early(weights, toks[:3], cots[:3])
    gate_delta, up_delta, hidden, route = forward_late(turn, weights, toks, cots, early)
    partial_sums = terms(gate_delta, up_delta, hidden, toks, cots, owners)
    summed = lax.psum_scatter(partial_sums, "dp", scatter_dimension=0, tiled=True)
    weight_grad = summed.astype(jnp.float32).transpose(0, 2, 1, 3)

    right = inputs(turn, gate_delta, up_delta, weights, route, half, half, 0)
    left = inputs(same, gate_delta, up_delta, weights, route, 0, half, EXTRA)
    left = spread(swap_blocks(small_turn, spread(left, "x", -1)), "z", -1)
    right = spread(swap_blocks(small_turn, spread(right, "z", -1)), "x", -1)

    def combine(blocks, code):
        return jnp.einsum(
            "ct,cd->td",
            one_hot(code, 0, ROWS),
            jnp.concatenate(blocks, axis=0),
            preferred_element_type=jnp.float32,
        ).astype(jnp.bfloat16)

    input_grad = jnp.concatenate(
        [combine([b[:, :half] for b in left], z_first), combine(right, x_first)], axis=1
    )
    route_mine = jnp.concatenate([b[:, half] for b in left], axis=0).astype(jnp.float32)
    row = lax.broadcasted_iota(jnp.int32, (ROWS, 1, 1), 0)
    route_grad = jnp.sum(jnp.where(row == z_first[None], route_mine[:, None, None], 0.0), axis=0)
    return input_grad, route_grad.astype(jnp.bfloat16).T, weight_grad


def solution(mesh):
    rows = P(("dp", "expert"), None)
    return jax.shard_map(
        shards,
        mesh=mesh,
        in_specs=(rows, rows, rows, rows, P("expert", None, None, None)),
        out_specs=(rows, rows, P("expert", "dp", None, None)),
        check_vma=False,
    )
```

```python
import functools

import jax
import jax.numpy as jnp
from jax import lax
from jax.experimental import pallas as pl
from jax.experimental.pallas import tpu as pltpu
from jax.sharding import PartitionSpec as P

CAP = 36
SIDE = 4
BLOCK = SIDE * CAP
ROWS = SIDE * BLOCK
EXTRA = 128
HOPS = (0, 1, 3, 2)
MAIN = 32
TAIL = CAP - MAIN
EARLY = 384
BIG = 56 << 20


def hop(dz, dx):
    return [
        (z * SIDE + x, (z + dz) % SIDE * SIDE + (x + dx) % SIDE)
        for z in range(SIDE)
        for x in range(SIDE)
    ]


def move(value, axis, step):
    if step % SIDE == 0:
        return value
    return lax.ppermute(value, "expert", hop(step, 0) if axis == "z" else hop(0, step))


def spread(blocks, axis, sign):
    return [move(blocks[p], axis, sign * HOPS[p]) for p in range(SIDE)]


def product(left, right, dims=((1,), (0,))):
    return lax.dot_general(left, right, (dims, ((), ())), preferred_element_type=jnp.float32)


def place(block, lane, slot):
    inner = jnp.where(slot < MAIN, lane * MAIN + slot, SIDE * MAIN + lane * TAIL + slot - MAIN)
    return block * BLOCK + inner


def swap_matrix(tails):
    size = SIDE * SIDE * TAIL if tails else ROWS
    row = jnp.arange(size, dtype=jnp.int32)
    if tails:
        source = row // TAIL % SIDE * SIDE * TAIL + row // TAIL // SIDE * TAIL + row % TAIL
    else:
        block, inner = row // BLOCK, row % BLOCK
        tail = inner - SIDE * MAIN
        lane = jnp.where(tail < 0, inner // MAIN, tail // TAIL)
        slot = jnp.where(tail < 0, inner % MAIN, MAIN + tail % TAIL)
        source = place(lane, block, slot)
    return (source[:, None] == row[None, :]).astype(jnp.bfloat16)


def params():
    return pltpu.CompilerParams(dimension_semantics=("arbitrary",), vmem_limit_bytes=BIG)


def cost(flops, moved):
    return pl.CostEstimate(flops=int(flops), bytes_accessed=int(moved), transcendentals=0)


def swap_near_kernel(*refs):
    ins, outs = refs[: SIDE - 1], refs[SIDE - 1 :]
    for p in range(SIDE - 1):
        for q in range(SIDE):
            outs[q][p * MAIN : (p + 1) * MAIN] = ins[p][q * MAIN : (q + 1) * MAIN]


def swap_far_kernel(matrix_ref, far_ref, *refs):
    near_tails, outs = refs[: SIDE - 1], refs[-SIDE:]
    far = far_ref[...]
    tails = jnp.concatenate([ref[...] for ref in near_tails] + [far[SIDE * MAIN :]], axis=0)
    tails = product(matrix_ref[...], tails).astype(jnp.bfloat16)
    for q in range(SIDE):
        outs[q][:MAIN] = far[q * MAIN : (q + 1) * MAIN]
        outs[q][MAIN:] = tails[q * SIDE * TAIL : (q + 1) * SIDE * TAIL]


def swap_blocks(matrix, blocks):
    width = blocks[0].shape[1]
    tile = width // 2 if width % 4096 == 0 else width
    grid = (width // tile,)
    shapes = [jax.ShapeDtypeStruct((BLOCK, width), jnp.bfloat16)] * SIDE
    last = SIDE - 1
    placed = pl.pallas_call(
        swap_near_kernel,
        grid=grid,
        in_specs=[pl.BlockSpec((SIDE * MAIN, tile), lambda i: (0, i))] * last,
        out_specs=[pl.BlockSpec((last * MAIN, tile), lambda i: (0, i))] * SIDE,
        out_shape=shapes,
        compiler_params=params(),
        cost_estimate=cost(0, 3 * ROWS * width),
        name="swap_near",
    )(*blocks[:last])
    left = BLOCK - last * MAIN
    tail = SIDE * TAIL
    return pl.pallas_call(
        swap_far_kernel,
        grid=grid,
        in_specs=[
            pl.BlockSpec(matrix.shape, lambda i: (0, 0)),
            pl.BlockSpec((BLOCK, tile), lambda i: (0, i)),
        ]
        + [pl.BlockSpec((tail, tile), lambda i: (BLOCK // tail - 1, i))] * last
        + [pl.BlockSpec(memory_space=pl.ANY)] * SIDE,
        out_specs=[pl.BlockSpec((left, tile), lambda i: (BLOCK // left - 1, i))] * SIDE,
        out_shape=shapes,
        input_output_aliases={2 + last + q: q for q in range(SIDE)},
        compiler_params=params(),
        cost_estimate=cost(2 * 64 * 64 * width, ROWS * width),
        name="swap_far",
    )(matrix, blocks[last], *blocks[:last], *placed)


LAST = ((1,), (1,))


def two(weight_ref):
    units, columns = weight_ref.shape[1:]
    return weight_ref[:2].reshape(2 * units, columns)


def early_kernel(weight_ref, *refs):
    toks, cots, outs = refs[0:3], refs[3:6], refs[6:8]

    @pl.when(pl.program_id(0) == 0)
    def _():
        for out in outs:
            out[...] = jnp.zeros_like(out)

    tok, cot = (
        jnp.concatenate([r[0][...], r[1][...], r[2][: EARLY - 2 * BLOCK]], axis=0)
        for r in (toks, cots)
    )
    both_out, back_out = outs
    both_out[...] += product(two(weight_ref), tok, LAST)
    back_out[...] += product(weight_ref[2], cot, LAST)


def forward_early(weights, toks, cots):
    units, width = weights.shape[1:]
    tile = 1024
    rows = pl.BlockSpec((BLOCK, tile), lambda i: (0, i))
    shapes = [(2 * units, EARLY), (units, EARLY)]
    return pl.pallas_call(
        early_kernel,
        grid=(width // tile,),
        in_specs=[pl.BlockSpec((3, units, tile), lambda i: (0, 0, i))] + [rows] * 6,
        out_specs=[pl.BlockSpec(shape, lambda i: (0, 0)) for shape in shapes],
        out_shape=[jax.ShapeDtypeStruct(shape, jnp.float32) for shape in shapes],
        compiler_params=params(),
        cost_estimate=cost(6 * EARLY * units * width, 6 * units * width + 4 * EARLY * width),
        name="forward_early",
    )(weights, *toks, *cots)


def late_kernel(steps, matrix_ref, weight_ref, *refs):
    toks, cots, scales = refs[0:2], refs[2:4], refs[4:8]
    early = refs[8:10]
    deltas_out, hidden_out, route_out = refs[10:13]
    accs = refs[13:15]
    step = pl.program_id(0)

    @pl.when(step == 0)
    def _():
        for acc in accs:
            acc[...] = jnp.zeros_like(acc)

    tok, cot = (
        jnp.concatenate([r[0][EARLY - 2 * BLOCK :], r[1][...]], axis=0) for r in (toks, cots)
    )
    accs[0][...] += product(two(weight_ref), tok, LAST)
    accs[1][...] += product(weight_ref[2], cot, LAST)

    @pl.when(step == steps - 1)
    def _():
        matrix = matrix_ref[...]
        both, back = (
            jnp.concatenate([first[...], acc[...]], axis=1) for first, acc in zip(early, accs)
        )
        units = back.shape[0]
        gate_pre, up_pre = both[:units], both[units:]
        lane = lax.broadcasted_iota(jnp.int32, (8, EXTRA), 1)
        first_lane = jnp.where(lane == 0, 1.0, 0.0).astype(jnp.bfloat16)
        scale = jnp.concatenate([ref[...] for ref in scales], axis=0)
        scale = product(first_lane, scale, LAST)[:1]
        grad = scale * back
        high = grad.astype(jnp.bfloat16)
        low = (grad - high.astype(jnp.float32)).astype(jnp.bfloat16)
        logistic = 1.0 / (1.0 + jnp.exp(-gate_pre))
        gated = gate_pre * logistic
        hidden = (gated * up_pre).astype(jnp.bfloat16)
        turned = product(jnp.concatenate([high, low, hidden], axis=0), matrix)
        grad = turned[:units] + turned[units : 2 * units]
        hidden = turned[2 * units :]
        hidden_out[...] = hidden.astype(jnp.bfloat16)
        deltas_out[:units] = (
            grad * up_pre * logistic * (1.0 + gate_pre * (1.0 - logistic))
        ).astype(jnp.bfloat16)
        deltas_out[units:] = (grad * gated).astype(jnp.bfloat16)
        route = jnp.sum(hidden * back, axis=0, keepdims=True).astype(jnp.bfloat16)
        route_out[...] = product(matrix, jnp.broadcast_to(route, (EXTRA, ROWS)), LAST).astype(
            jnp.bfloat16
        )


def forward_late(matrix, weights, toks, cots, early):
    units, width = weights.shape[1:]
    tile = 1024
    steps = width // tile
    rows = pl.BlockSpec((BLOCK, tile), lambda i: (0, i))
    extra = pl.BlockSpec((BLOCK, EXTRA), lambda i: (0, width // EXTRA))
    shapes = [(2 * units, ROWS), (units, ROWS), (ROWS, EXTRA)]
    late = ROWS - EARLY
    return pl.pallas_call(
        functools.partial(late_kernel, steps),
        grid=(steps,),
        in_specs=[
            pl.BlockSpec((ROWS, ROWS), lambda i: (0, 0)),
            pl.BlockSpec((3, units, tile), lambda i: (0, 0, i)),
        ]
        + [rows] * 4
        + [extra] * 4
        + [pl.BlockSpec(array.shape, lambda i: (0, 0)) for array in early],
        out_specs=[pl.BlockSpec(shape, lambda i: (0, 0)) for shape in shapes],
        out_shape=[jax.ShapeDtypeStruct(shape, jnp.bfloat16) for shape in shapes],
        scratch_shapes=[pltpu.VMEM((n * units, late), jnp.float32) for n in (2, 1)],
        compiler_params=params(),
        cost_estimate=cost(6 * late * units * width, 6 * units * width + 12 * EARLY * units),
        name="forward_late",
    )(matrix, weights, *toks[2:], *cots[2:], *cots, *early)


def terms_kernel(deltas_ref, hidden_ref, *refs):
    toks, cots, scales, out_ref = refs[0:4], refs[4:8], refs[8:12], refs[12]
    tok = jnp.concatenate([ref[...] for ref in toks], axis=0)
    scaled = jnp.concatenate(
        [
            (ref[...].astype(jnp.float32) * scale[:, :1].astype(jnp.float32)).astype(jnp.bfloat16)
            for ref, scale in zip(cots, scales)
        ],
        axis=0,
    )
    share = out_ref.shape[2]
    units = hidden_ref.shape[0]
    kind = 0
    for left, right in ((deltas_ref, tok), (hidden_ref, scaled)):
        term = product(left[...], right)
        for first in range(0, left.shape[0], units):
            for owner in range(units // share):
                rows = term[first + owner * share : first + (owner + 1) * share]
                out_ref[owner, kind] = rows.astype(jnp.bfloat16)
            kind += 1


def terms(deltas, hidden, toks, cots, owners):
    units = hidden.shape[0]
    width = toks[0].shape[1]
    tile = 1024
    rows = pl.BlockSpec((BLOCK, tile), lambda i: (0, i))
    extra = pl.BlockSpec((BLOCK, EXTRA), lambda i: (0, width // EXTRA))
    share = units // owners
    return pl.pallas_call(
        terms_kernel,
        grid=(width // tile,),
        in_specs=[pl.BlockSpec(array.shape, lambda i: (0, 0)) for array in (deltas, hidden)]
        + [rows] * 8
        + [extra] * 4,
        out_specs=pl.BlockSpec((owners, 3, share, tile), lambda i: (0, 0, 0, i)),
        out_shape=jax.ShapeDtypeStruct((owners, 3, share, width), jnp.bfloat16),
        compiler_params=params(),
        cost_estimate=cost(6 * ROWS * units * width, 6 * units * width + 4 * ROWS * width),
        name="terms",
    )(deltas, hidden, *toks, *cots, *cots)


def inputs_kernel(tile, turn_ref, deltas_ref, weight_ref, route_ref, *refs):
    outs, delta_rows = refs[:SIDE], refs[SIDE]
    step = pl.program_id(0)

    @pl.when(step == 0)
    def _():
        delta_rows[...] = product(turn_ref[...], deltas_ref[...], LAST).astype(jnp.bfloat16)
        for p in range(SIDE):
            width = outs[p].shape[1]
            if width % tile:
                outs[p][:, width - EXTRA :] = route_ref[p * BLOCK : (p + 1) * BLOCK]

    value = product(delta_rows[...], two(weight_ref)).astype(jnp.bfloat16)
    columns = pl.ds(pl.multiple_of(step * tile, tile), tile)
    for p in range(SIDE):
        outs[p][:, columns] = value[p * BLOCK : (p + 1) * BLOCK]


def inputs(turn, deltas, weights, route, first, count, extra):
    units = weights.shape[1]
    tile = 512
    block = (BLOCK, count + extra)
    return pl.pallas_call(
        functools.partial(inputs_kernel, tile),
        grid=(count // tile,),
        in_specs=[
            pl.BlockSpec((ROWS, ROWS), lambda i: (0, 0)),
            pl.BlockSpec((2 * units, ROWS), lambda i: (0, 0)),
            pl.BlockSpec((2, units, tile), lambda i: (0, 0, first // tile + i)),
            pl.BlockSpec((ROWS, EXTRA), lambda i: (0, 0)),
        ],
        out_specs=[pl.BlockSpec(block, lambda i: (0, 0))] * SIDE,
        out_shape=[jax.ShapeDtypeStruct(block, jnp.bfloat16)] * SIDE,
        scratch_shapes=[pltpu.VMEM((ROWS, 2 * units), jnp.bfloat16)],
        compiler_params=params(),
        cost_estimate=cost(4 * ROWS * units * count, 4 * units * count + 2 * ROWS * count),
        name="inputs",
    )(turn, deltas, weights, route)


def shards(tokens, cotangent, expert_ids, route_weights, expert_weights):
    me = lax.axis_index("expert")
    z, x = me // SIDE, me % SIDE
    tok_rows, width = tokens.shape
    half = width // 2
    experts = SIDE * SIDE
    owners = lax.axis_size("dp")

    ids = expert_ids.T
    column = lax.broadcasted_iota(jnp.int32, (experts, 1, 1), 0)
    named = ids[None] == column
    routed = jnp.any(named, axis=1)
    earlier = (
        lax.broadcasted_iota(jnp.int32, (tok_rows, tok_rows), 0)
        < lax.broadcasted_iota(jnp.int32, (tok_rows, tok_rows), 1)
    ).astype(jnp.bfloat16)
    slots = jnp.dot(routed.astype(jnp.bfloat16), earlier, preferred_element_type=jnp.float32)
    slots = slots.astype(jnp.int32)
    expert = lax.broadcasted_iota(jnp.int32, (experts, 1), 0)
    far_z, far_x = (expert // SIDE - z) % SIDE, (expert % SIDE - x) % SIDE
    near_z = jnp.where(far_z >= 2, 5 - far_z, far_z)
    near_x = jnp.where(far_x >= 2, 5 - far_x, far_x)
    live = jnp.any(named, axis=0)

    def codes(block, lane):
        row = place(block, lane, slots)
        return jnp.where(live, jnp.sum(jnp.where(named, row[:, None, :], 0), axis=0), -1)

    def one_hot(code, first, count):
        row = lax.broadcasted_iota(jnp.int32, (count, tok_rows), 0) + first
        hot = row == code[0][None, :]
        for k in range(1, code.shape[0]):
            hot = hot | (row == code[k][None, :])
        return hot.astype(jnp.bfloat16)

    z_first = codes(near_z, near_x)
    x_first = codes(near_x, near_z)

    def row_scales(code, first):
        row = lax.broadcasted_iota(jnp.int32, (BLOCK, 1, 1), 0) + first
        scale = jnp.where(row == code[None], route_weights.T[None], 0.0)
        return jnp.sum(scale, axis=(1, 2))[:, None].astype(jnp.bfloat16)

    def pick(left, right):
        return jnp.dot(left, right, preferred_element_type=jnp.float32).astype(jnp.bfloat16)

    tok_blocks, cot_blocks = [], []
    for p in range(SIDE):
        tok_blocks.append(pick(one_hot(z_first, p * BLOCK, BLOCK), tokens))
        picked = pick(one_hot(x_first, p * BLOCK, BLOCK), cotangent)
        scale = jnp.broadcast_to(row_scales(x_first, p * BLOCK), (BLOCK, EXTRA))
        cot_blocks.append(jnp.concatenate([picked, scale], axis=1))

    turn = swap_matrix(False)
    small_turn = swap_matrix(True)
    same = (jnp.arange(ROWS)[:, None] == jnp.arange(ROWS)[None, :]).astype(jnp.bfloat16)

    def near_then_far(blocks, axis):
        near = [blocks[0]] + [move(blocks[p], axis, HOPS[p]) for p in (1, 2)]
        far = lax.optimization_barrier((blocks[3], near[1], near[2]))
        return [near[0], far[1], far[2], move(far[0], axis, HOPS[3])]

    toks = near_then_far(swap_blocks(small_turn, near_then_far(tok_blocks, "z")), "x")
    cots = near_then_far(swap_blocks(small_turn, near_then_far(cot_blocks, "x")), "z")

    weights = expert_weights[0].transpose(1, 0, 2)
    early = forward_early(weights, toks[:3], cots[:3])
    deltas, hidden, route = forward_late(turn, weights, toks, cots, early)
    partial_sums = terms(deltas, hidden, toks, cots, owners)
    summed = lax.psum_scatter(partial_sums, "dp", scatter_dimension=0, tiled=True)
    weight_grad = summed.astype(jnp.float32).transpose(0, 2, 1, 3)

    right = inputs(turn, deltas, weights, route, half, half, 0)
    left = inputs(same, deltas, weights, route, 0, half, EXTRA)
    left = spread(swap_blocks(small_turn, spread(left, "x", -1)), "z", -1)
    right = spread(swap_blocks(small_turn, spread(right, "z", -1)), "x", -1)

    def combine(blocks, code):
        return jnp.einsum(
            "ct,cd->td",
            one_hot(code, 0, ROWS),
            jnp.concatenate(blocks, axis=0),
            preferred_element_type=jnp.float32,
        ).astype(jnp.bfloat16)

    input_grad = jnp.concatenate(
        [combine([b[:, :half] for b in left], z_first), combine(right, x_first)], axis=1
    )
    route_mine = jnp.concatenate([b[:, half] for b in left], axis=0).astype(jnp.float32)
    row = lax.broadcasted_iota(jnp.int32, (ROWS, 1, 1), 0)
    route_grad = jnp.sum(jnp.where(row == z_first[None], route_mine[:, None, None], 0.0), axis=0)
    return input_grad, route_grad.astype(jnp.bfloat16).T, weight_grad


def solution(mesh):
    rows = P(("dp", "expert"), None)
    return jax.shard_map(
        shards,
        mesh=mesh,
        in_specs=(rows, rows, rows, rows, P("expert", None, None, None)),
        out_specs=(rows, rows, P("expert", "dp", None, None)),
        check_vma=False,
    )
```

```python
import functools

import jax
import jax.numpy as jnp
from jax import lax
from jax.experimental import pallas as pl
from jax.experimental.pallas import tpu as pltpu
from jax.sharding import PartitionSpec as P

CAP = 36
SIDE = 4
BLOCK = SIDE * CAP
ROWS = SIDE * BLOCK
EXTRA = 128
HOPS = (0, 1, 3, 2)
MAIN = 32
TAIL = CAP - MAIN
EARLY = 384
LIMITS = {"swap": 16, "early": 16, "late": 16, "terms": 16, "inputs": 16, "widen": 56}


def hop(dz, dx):
    return [
        (z * SIDE + x, (z + dz) % SIDE * SIDE + (x + dx) % SIDE)
        for z in range(SIDE)
        for x in range(SIDE)
    ]


def move(value, axis, step):
    if step % SIDE == 0:
        return value
    return lax.ppermute(value, "expert", hop(step, 0) if axis == "z" else hop(0, step))


def spread(blocks, axis, sign):
    return [move(blocks[p], axis, sign * HOPS[p]) for p in range(SIDE)]


def product(left, right, dims=((1,), (0,))):
    return lax.dot_general(left, right, (dims, ((), ())), preferred_element_type=jnp.float32)


def place(block, lane, slot):
    inner = jnp.where(slot < MAIN, lane * MAIN + slot, SIDE * MAIN + lane * TAIL + slot - MAIN)
    return block * BLOCK + inner


def swap_matrix(tails):
    size = SIDE * SIDE * TAIL if tails else ROWS
    row = jnp.arange(size, dtype=jnp.int32)
    if tails:
        source = row // TAIL % SIDE * SIDE * TAIL + row // TAIL // SIDE * TAIL + row % TAIL
    else:
        block, inner = row // BLOCK, row % BLOCK
        tail = inner - SIDE * MAIN
        lane = jnp.where(tail < 0, inner // MAIN, tail // TAIL)
        slot = jnp.where(tail < 0, inner % MAIN, MAIN + tail % TAIL)
        source = place(lane, block, slot)
    return (source[:, None] == row[None, :]).astype(jnp.bfloat16)


def params(kernel):
    return pltpu.CompilerParams(
        dimension_semantics=("arbitrary",), vmem_limit_bytes=LIMITS[kernel] << 20
    )


def cost(flops, moved):
    return pl.CostEstimate(flops=int(flops), bytes_accessed=int(moved), transcendentals=0)


def swap_near_kernel(*refs):
    ins, outs = refs[: SIDE - 1], refs[SIDE - 1 :]
    for p in range(SIDE - 1):
        for q in range(SIDE):
            outs[q][p * MAIN : (p + 1) * MAIN] = ins[p][q * MAIN : (q + 1) * MAIN]


def swap_far_kernel(matrix_ref, far_ref, *refs):
    near_tails, outs = refs[: SIDE - 1], refs[-SIDE:]
    far = far_ref[...]
    tails = jnp.concatenate([ref[...] for ref in near_tails] + [far[SIDE * MAIN :]], axis=0)
    tails = product(matrix_ref[...], tails).astype(jnp.bfloat16)
    for q in range(SIDE):
        outs[q][:MAIN] = far[q * MAIN : (q + 1) * MAIN]
        outs[q][MAIN:] = tails[q * SIDE * TAIL : (q + 1) * SIDE * TAIL]


def swap_blocks(matrix, blocks):
    width = blocks[0].shape[1]
    tile = width // 2 if width % 4096 == 0 else width
    grid = (width // tile,)
    shapes = [jax.ShapeDtypeStruct((BLOCK, width), jnp.bfloat16)] * SIDE
    last = SIDE - 1
    placed = pl.pallas_call(
        swap_near_kernel,
        grid=grid,
        in_specs=[pl.BlockSpec((SIDE * MAIN, tile), lambda i: (0, i))] * last,
        out_specs=[pl.BlockSpec((last * MAIN, tile), lambda i: (0, i))] * SIDE,
        out_shape=shapes,
        compiler_params=params("swap"),
        cost_estimate=cost(0, 3 * ROWS * width),
        name="swap_near",
    )(*blocks[:last])
    left = BLOCK - last * MAIN
    tail = SIDE * TAIL
    return pl.pallas_call(
        swap_far_kernel,
        grid=grid,
        in_specs=[
            pl.BlockSpec(matrix.shape, lambda i: (0, 0)),
            pl.BlockSpec((BLOCK, tile), lambda i: (0, i)),
        ]
        + [pl.BlockSpec((tail, tile), lambda i: (BLOCK // tail - 1, i))] * last
        + [pl.BlockSpec(memory_space=pl.ANY)] * SIDE,
        out_specs=[pl.BlockSpec((left, tile), lambda i: (BLOCK // left - 1, i))] * SIDE,
        out_shape=shapes,
        input_output_aliases={2 + last + q: q for q in range(SIDE)},
        compiler_params=params("swap"),
        cost_estimate=cost(2 * 64 * 64 * width, ROWS * width),
        name="swap_far",
    )(matrix, blocks[last], *blocks[:last], *placed)


LAST = ((1,), (1,))


def two(weight_ref):
    units, columns = weight_ref.shape[1:]
    return weight_ref[:2].reshape(2 * units, columns)


def early_kernel(weight_ref, *refs):
    toks, cots, outs = refs[0:3], refs[3:6], refs[6:8]

    @pl.when(pl.program_id(0) == 0)
    def _():
        for out in outs:
            out[...] = jnp.zeros_like(out)

    tok, cot = (
        jnp.concatenate([r[0][...], r[1][...], r[2][: EARLY - 2 * BLOCK]], axis=0)
        for r in (toks, cots)
    )
    both_out, back_out = outs
    both_out[...] += product(two(weight_ref), tok, LAST)
    back_out[...] += product(weight_ref[2], cot, LAST)


def forward_early(weights, toks, cots):
    units, width = weights.shape[1:]
    tile = 512
    rows = pl.BlockSpec((BLOCK, tile), lambda i: (0, i))
    shapes = [(2 * units, EARLY), (units, EARLY)]
    return pl.pallas_call(
        early_kernel,
        grid=(width // tile,),
        in_specs=[pl.BlockSpec((3, units, tile), lambda i: (0, 0, i))] + [rows] * 6,
        out_specs=[pl.BlockSpec(shape, lambda i: (0, 0)) for shape in shapes],
        out_shape=[jax.ShapeDtypeStruct(shape, jnp.float32) for shape in shapes],
        compiler_params=params("early"),
        cost_estimate=cost(6 * EARLY * units * width, 6 * units * width + 4 * EARLY * width),
        name="forward_early",
    )(weights, *toks, *cots)


def late_kernel(steps, matrix_ref, weight_ref, *refs):
    toks, cots, scales = refs[0:2], refs[2:4], refs[4:8]
    early = refs[8:10]
    deltas_out, hidden_out, route_out = refs[10:13]
    accs = refs[13:15]
    step = pl.program_id(0)

    @pl.when(step == 0)
    def _():
        for acc in accs:
            acc[...] = jnp.zeros_like(acc)

    tok, cot = (
        jnp.concatenate([r[0][EARLY - 2 * BLOCK :], r[1][...]], axis=0) for r in (toks, cots)
    )
    accs[0][...] += product(two(weight_ref), tok, LAST)
    accs[1][...] += product(weight_ref[2], cot, LAST)

    @pl.when(step == steps - 1)
    def _():
        matrix = matrix_ref[...]
        both, back = (
            jnp.concatenate([first[...], acc[...]], axis=1) for first, acc in zip(early, accs)
        )
        units = back.shape[0]
        gate_pre, up_pre = both[:units], both[units:]
        lane = lax.broadcasted_iota(jnp.int32, (8, EXTRA), 1)
        first_lane = jnp.where(lane == 0, 1.0, 0.0).astype(jnp.bfloat16)
        scale = jnp.concatenate([ref[...] for ref in scales], axis=0)
        scale = product(first_lane, scale, LAST)[:1]
        grad = scale * back
        high = grad.astype(jnp.bfloat16)
        low = (grad - high.astype(jnp.float32)).astype(jnp.bfloat16)
        logistic = 1.0 / (1.0 + jnp.exp(-gate_pre))
        gated = gate_pre * logistic
        hidden = (gated * up_pre).astype(jnp.bfloat16)
        turned = product(jnp.concatenate([high, low, hidden], axis=0), matrix)
        grad = turned[:units] + turned[units : 2 * units]
        hidden = turned[2 * units :]
        hidden_out[...] = hidden.astype(jnp.bfloat16)
        deltas_out[:units] = (
            grad * up_pre * logistic * (1.0 + gate_pre * (1.0 - logistic))
        ).astype(jnp.bfloat16)
        deltas_out[units:] = (grad * gated).astype(jnp.bfloat16)
        route = jnp.sum(hidden * back, axis=0, keepdims=True).astype(jnp.bfloat16)
        route_out[...] = product(matrix, jnp.broadcast_to(route, (EXTRA, ROWS)), LAST).astype(
            jnp.bfloat16
        )


def forward_late(matrix, weights, toks, cots, early):
    units, width = weights.shape[1:]
    tile = 512
    steps = width // tile
    rows = pl.BlockSpec((BLOCK, tile), lambda i: (0, i))
    extra = pl.BlockSpec((BLOCK, EXTRA), lambda i: (0, width // EXTRA))
    shapes = [(2 * units, ROWS), (units, ROWS), (ROWS, EXTRA)]
    late = ROWS - EARLY
    return pl.pallas_call(
        functools.partial(late_kernel, steps),
        grid=(steps,),
        in_specs=[
            pl.BlockSpec((ROWS, ROWS), lambda i: (0, 0)),
            pl.BlockSpec((3, units, tile), lambda i: (0, 0, i)),
        ]
        + [rows] * 4
        + [extra] * 4
        + [pl.BlockSpec(array.shape, lambda i: (0, 0)) for array in early],
        out_specs=[pl.BlockSpec(shape, lambda i: (0, 0)) for shape in shapes],
        out_shape=[jax.ShapeDtypeStruct(shape, jnp.bfloat16) for shape in shapes],
        scratch_shapes=[pltpu.VMEM((n * units, late), jnp.float32) for n in (2, 1)],
        compiler_params=params("late"),
        cost_estimate=cost(6 * late * units * width, 6 * units * width + 12 * EARLY * units),
        name="forward_late",
    )(matrix, weights, *toks[2:], *cots[2:], *cots, *early)


def terms_kernel(deltas_ref, hidden_ref, *refs):
    toks, cots, scales, out_ref = refs[0:4], refs[4:8], refs[8:12], refs[12]
    tok = jnp.concatenate([ref[...] for ref in toks], axis=0)
    scaled = jnp.concatenate(
        [
            (ref[...].astype(jnp.float32) * scale[:, :1].astype(jnp.float32)).astype(jnp.bfloat16)
            for ref, scale in zip(cots, scales)
        ],
        axis=0,
    )
    share = out_ref.shape[2]
    units = hidden_ref.shape[0]
    kind = 0
    for left, right in ((deltas_ref, tok), (hidden_ref, scaled)):
        term = product(left[...], right)
        for first in range(0, left.shape[0], units):
            for owner in range(units // share):
                rows = term[first + owner * share : first + (owner + 1) * share]
                out_ref[owner, kind] = rows.astype(jnp.bfloat16)
            kind += 1


def terms(deltas, hidden, toks, cots, owners):
    units = hidden.shape[0]
    width = toks[0].shape[1]
    tile = 512
    rows = pl.BlockSpec((BLOCK, tile), lambda i: (0, i))
    extra = pl.BlockSpec((BLOCK, EXTRA), lambda i: (0, width // EXTRA))
    share = units // owners
    return pl.pallas_call(
        terms_kernel,
        grid=(width // tile,),
        in_specs=[pl.BlockSpec(array.shape, lambda i: (0, 0)) for array in (deltas, hidden)]
        + [rows] * 8
        + [extra] * 4,
        out_specs=pl.BlockSpec((owners, 3, share, tile), lambda i: (0, 0, 0, i)),
        out_shape=pltpu.HBM((owners, 3, share, width), jnp.bfloat16),
        compiler_params=params("terms"),
        cost_estimate=cost(6 * ROWS * units * width, 6 * units * width + 4 * ROWS * width),
        name="terms",
    )(deltas, hidden, *toks, *cots, *cots)


def widen_kernel(in_ref, out_ref):
    out_ref[0, 0] = in_ref[0, 0].astype(jnp.float32)


def widen(summed):
    _, kinds, share, width = summed.shape
    tile = width // 2
    spec = pl.BlockSpec((1, 1, share, tile), lambda i: (0, i // 2, 0, i % 2))
    return pl.pallas_call(
        widen_kernel,
        grid=(2 * kinds,),
        in_specs=[spec],
        out_specs=spec,
        out_shape=jax.ShapeDtypeStruct(summed.shape, jnp.float32),
        compiler_params=params("widen"),
        cost_estimate=cost(0, 6 * kinds * share * width),
        name="widen",
    )(summed)


def inputs_kernel(tile, turn_ref, deltas_ref, weight_ref, route_ref, *refs):
    outs, delta_rows = refs[:SIDE], refs[SIDE]
    step = pl.program_id(0)

    @pl.when(step == 0)
    def _():
        delta_rows[...] = product(turn_ref[...], deltas_ref[...], LAST).astype(jnp.bfloat16)
        for p in range(SIDE):
            width = outs[p].shape[1]
            if width % tile:
                outs[p][:, width - EXTRA :] = route_ref[p * BLOCK : (p + 1) * BLOCK]

    value = product(delta_rows[...], two(weight_ref)).astype(jnp.bfloat16)
    columns = pl.ds(pl.multiple_of(step * tile, tile), tile)
    for p in range(SIDE):
        outs[p][:, columns] = value[p * BLOCK : (p + 1) * BLOCK]


def inputs(turn, deltas, weights, route, first, count, extra):
    units = weights.shape[1]
    tile = 512
    block = (BLOCK, count + extra)
    return pl.pallas_call(
        functools.partial(inputs_kernel, tile),
        grid=(count // tile,),
        in_specs=[
            pl.BlockSpec((ROWS, ROWS), lambda i: (0, 0)),
            pl.BlockSpec((2 * units, ROWS), lambda i: (0, 0)),
            pl.BlockSpec((2, units, tile), lambda i: (0, 0, first // tile + i)),
            pl.BlockSpec((ROWS, EXTRA), lambda i: (0, 0)),
        ],
        out_specs=[pl.BlockSpec(block, lambda i: (0, 0))] * SIDE,
        out_shape=[jax.ShapeDtypeStruct(block, jnp.bfloat16)] * SIDE,
        scratch_shapes=[pltpu.VMEM((ROWS, 2 * units), jnp.bfloat16)],
        compiler_params=params("inputs"),
        cost_estimate=cost(4 * ROWS * units * count, 4 * units * count + 2 * ROWS * count),
        name="inputs",
    )(turn, deltas, weights, route)


def shards(tokens, cotangent, expert_ids, route_weights, expert_weights):
    me = lax.axis_index("expert")
    z, x = me // SIDE, me % SIDE
    tok_rows, width = tokens.shape
    half = width // 2
    experts = SIDE * SIDE
    owners = lax.axis_size("dp")

    ids = expert_ids.T
    column = lax.broadcasted_iota(jnp.int32, (experts, 1, 1), 0)
    named = ids[None] == column
    routed = jnp.any(named, axis=1)
    earlier = (
        lax.broadcasted_iota(jnp.int32, (tok_rows, tok_rows), 0)
        < lax.broadcasted_iota(jnp.int32, (tok_rows, tok_rows), 1)
    ).astype(jnp.bfloat16)
    slots = jnp.dot(routed.astype(jnp.bfloat16), earlier, preferred_element_type=jnp.float32)
    slots = slots.astype(jnp.int32)
    expert = lax.broadcasted_iota(jnp.int32, (experts, 1), 0)
    far_z, far_x = (expert // SIDE - z) % SIDE, (expert % SIDE - x) % SIDE
    near_z = jnp.where(far_z >= 2, 5 - far_z, far_z)
    near_x = jnp.where(far_x >= 2, 5 - far_x, far_x)
    live = jnp.any(named, axis=0)

    def codes(block, lane):
        row = place(block, lane, slots)
        return jnp.where(live, jnp.sum(jnp.where(named, row[:, None, :], 0), axis=0), -1)

    def one_hot(code, first, count):
        row = lax.broadcasted_iota(jnp.int32, (count, tok_rows), 0) + first
        hot = row == code[0][None, :]
        for k in range(1, code.shape[0]):
            hot = hot | (row == code[k][None, :])
        return hot.astype(jnp.bfloat16)

    z_first = codes(near_z, near_x)
    x_first = codes(near_x, near_z)

    def row_scales(code, first):
        row = lax.broadcasted_iota(jnp.int32, (BLOCK, 1, 1), 0) + first
        scale = jnp.where(row == code[None], route_weights.T[None], 0.0)
        return jnp.sum(scale, axis=(1, 2))[:, None].astype(jnp.bfloat16)

    def pick(left, right):
        return jnp.dot(left, right, preferred_element_type=jnp.float32).astype(jnp.bfloat16)

    tok_blocks, cot_blocks = [], []
    for p in range(SIDE):
        tok_blocks.append(pick(one_hot(z_first, p * BLOCK, BLOCK), tokens))
        picked = pick(one_hot(x_first, p * BLOCK, BLOCK), cotangent)
        scale = jnp.broadcast_to(row_scales(x_first, p * BLOCK), (BLOCK, EXTRA))
        cot_blocks.append(jnp.concatenate([picked, scale], axis=1))

    turn = swap_matrix(False)
    small_turn = swap_matrix(True)
    same = (jnp.arange(ROWS)[:, None] == jnp.arange(ROWS)[None, :]).astype(jnp.bfloat16)

    def near_then_far(blocks, axis):
        near = [blocks[0]] + [move(blocks[p], axis, HOPS[p]) for p in (1, 2)]
        far = lax.optimization_barrier((blocks[3], near[1], near[2]))
        return [near[0], far[1], far[2], move(far[0], axis, HOPS[3])]

    toks = near_then_far(swap_blocks(small_turn, near_then_far(tok_blocks, "z")), "x")
    cots = near_then_far(swap_blocks(small_turn, near_then_far(cot_blocks, "x")), "z")

    weights = expert_weights[0].transpose(1, 0, 2)
    early = forward_early(weights, toks[:3], cots[:3])
    deltas, hidden, route = forward_late(turn, weights, toks, cots, early)
    partial_sums = terms(deltas, hidden, toks, cots, owners)
    summed = lax.psum_scatter(partial_sums, "dp", scatter_dimension=0, tiled=True)
    weight_grad = widen(summed).transpose(0, 2, 1, 3)

    right = inputs(turn, deltas, weights, route, half, half, 0)
    left = inputs(same, deltas, weights, route, 0, half, EXTRA)
    left = spread(swap_blocks(small_turn, spread(left, "x", -1)), "z", -1)
    right = spread(swap_blocks(small_turn, spread(right, "z", -1)), "x", -1)

    def combine(blocks, code):
        return jnp.einsum(
            "ct,cd->td",
            one_hot(code, 0, ROWS),
            jnp.concatenate(blocks, axis=0),
            preferred_element_type=jnp.float32,
        ).astype(jnp.bfloat16)

    input_grad = jnp.concatenate(
        [combine([b[:, :half] for b in left], z_first), combine(right, x_first)], axis=1
    )
    route_mine = jnp.concatenate([b[:, half] for b in left], axis=0).astype(jnp.float32)
    row = lax.broadcasted_iota(jnp.int32, (ROWS, 1, 1), 0)
    route_grad = jnp.sum(jnp.where(row == z_first[None], route_mine[:, None, None], 0.0), axis=0)
    return input_grad, route_grad.astype(jnp.bfloat16).T, weight_grad


def solution(mesh):
    rows = P(("dp", "expert"), None)
    return jax.shard_map(
        shards,
        mesh=mesh,
        in_specs=(rows, rows, rows, rows, P("expert", None, None, None)),
        out_specs=(rows, rows, P("expert", "dp", None, None)),
        check_vma=False,
    )
```

```python
import functools

import jax
import jax.numpy as jnp
from jax import lax
from jax.experimental import pallas as pl
from jax.experimental.pallas import tpu as pltpu
from jax.sharding import PartitionSpec as P

CAP = 36
SIDE = 4
BLOCK = SIDE * CAP
ROWS = SIDE * BLOCK
EXTRA = 128
HOPS = (0, 1, 3, 2)
MAIN = 32
TAIL = CAP - MAIN
EARLY = 384
LIMITS = {"swap": 16, "early": 16, "late": 16, "terms": 16, "inputs": 16}


def hop(dz, dx):
    return [
        (z * SIDE + x, (z + dz) % SIDE * SIDE + (x + dx) % SIDE)
        for z in range(SIDE)
        for x in range(SIDE)
    ]


def move(value, axis, step):
    if step % SIDE == 0:
        return value
    return lax.ppermute(value, "expert", hop(step, 0) if axis == "z" else hop(0, step))


def spread(blocks, axis, sign):
    return [move(blocks[p], axis, sign * HOPS[p]) for p in range(SIDE)]


def product(left, right, dims=((1,), (0,))):
    return lax.dot_general(left, right, (dims, ((), ())), preferred_element_type=jnp.float32)


def place(block, lane, slot):
    inner = jnp.where(slot < MAIN, lane * MAIN + slot, SIDE * MAIN + lane * TAIL + slot - MAIN)
    return block * BLOCK + inner


def swap_matrix(tails):
    size = SIDE * SIDE * TAIL if tails else ROWS
    row = jnp.arange(size, dtype=jnp.int32)
    if tails:
        source = row // TAIL % SIDE * SIDE * TAIL + row // TAIL // SIDE * TAIL + row % TAIL
    else:
        block, inner = row // BLOCK, row % BLOCK
        tail = inner - SIDE * MAIN
        lane = jnp.where(tail < 0, inner // MAIN, tail // TAIL)
        slot = jnp.where(tail < 0, inner % MAIN, MAIN + tail % TAIL)
        source = place(lane, block, slot)
    return (source[:, None] == row[None, :]).astype(jnp.bfloat16)


def params(kernel):
    return pltpu.CompilerParams(
        dimension_semantics=("arbitrary",), vmem_limit_bytes=LIMITS[kernel] << 20
    )


def cost(flops, moved):
    return pl.CostEstimate(flops=int(flops), bytes_accessed=int(moved), transcendentals=0)


def swap_near_kernel(*refs):
    ins, outs = refs[: SIDE - 1], refs[SIDE - 1 :]
    for p in range(SIDE - 1):
        for q in range(SIDE):
            outs[q][p * MAIN : (p + 1) * MAIN] = ins[p][q * MAIN : (q + 1) * MAIN]


def swap_far_kernel(matrix_ref, far_ref, *refs):
    near_tails, outs = refs[: SIDE - 1], refs[-SIDE:]
    far = far_ref[...]
    tails = jnp.concatenate([ref[...] for ref in near_tails] + [far[SIDE * MAIN :]], axis=0)
    tails = product(matrix_ref[...], tails).astype(jnp.bfloat16)
    for q in range(SIDE):
        outs[q][:MAIN] = far[q * MAIN : (q + 1) * MAIN]
        outs[q][MAIN:] = tails[q * SIDE * TAIL : (q + 1) * SIDE * TAIL]


def swap_blocks(matrix, blocks):
    width = blocks[0].shape[1]
    tile = width // 2 if width % 4096 == 0 else width
    grid = (width // tile,)
    shapes = [jax.ShapeDtypeStruct((BLOCK, width), jnp.bfloat16)] * SIDE
    last = SIDE - 1
    placed = pl.pallas_call(
        swap_near_kernel,
        grid=grid,
        in_specs=[pl.BlockSpec((SIDE * MAIN, tile), lambda i: (0, i))] * last,
        out_specs=[pl.BlockSpec((last * MAIN, tile), lambda i: (0, i))] * SIDE,
        out_shape=shapes,
        compiler_params=params("swap"),
        cost_estimate=cost(0, 3 * ROWS * width),
        name="swap_near",
    )(*blocks[:last])
    left = BLOCK - last * MAIN
    tail = SIDE * TAIL
    return pl.pallas_call(
        swap_far_kernel,
        grid=grid,
        in_specs=[
            pl.BlockSpec(matrix.shape, lambda i: (0, 0)),
            pl.BlockSpec((BLOCK, tile), lambda i: (0, i)),
        ]
        + [pl.BlockSpec((tail, tile), lambda i: (BLOCK // tail - 1, i))] * last
        + [pl.BlockSpec(memory_space=pl.ANY)] * SIDE,
        out_specs=[pl.BlockSpec((left, tile), lambda i: (BLOCK // left - 1, i))] * SIDE,
        out_shape=shapes,
        input_output_aliases={2 + last + q: q for q in range(SIDE)},
        compiler_params=params("swap"),
        cost_estimate=cost(2 * 64 * 64 * width, ROWS * width),
        name="swap_far",
    )(matrix, blocks[last], *blocks[:last], *placed)


LAST = ((1,), (1,))


def two(weight_ref):
    units, columns = weight_ref.shape[1:]
    return weight_ref[:2].reshape(2 * units, columns)


def early_kernel(weight_ref, *refs):
    toks, cots, outs = refs[0:3], refs[3:6], refs[6:8]

    @pl.when(pl.program_id(0) == 0)
    def _():
        for out in outs:
            out[...] = jnp.zeros_like(out)

    tok, cot = (
        jnp.concatenate([r[0][...], r[1][...], r[2][: EARLY - 2 * BLOCK]], axis=0)
        for r in (toks, cots)
    )
    both_out, back_out = outs
    both_out[...] += product(two(weight_ref), tok, LAST)
    back_out[...] += product(weight_ref[2], cot, LAST)


def forward_early(weights, toks, cots):
    units, width = weights.shape[1:]
    tile = 512
    rows = pl.BlockSpec((BLOCK, tile), lambda i: (0, i))
    shapes = [(2 * units, EARLY), (units, EARLY)]
    return pl.pallas_call(
        early_kernel,
        grid=(width // tile,),
        in_specs=[pl.BlockSpec((3, units, tile), lambda i: (0, 0, i))] + [rows] * 6,
        out_specs=[pl.BlockSpec(shape, lambda i: (0, 0)) for shape in shapes],
        out_shape=[jax.ShapeDtypeStruct(shape, jnp.float32) for shape in shapes],
        compiler_params=params("early"),
        cost_estimate=cost(6 * EARLY * units * width, 6 * units * width + 4 * EARLY * width),
        name="forward_early",
    )(weights, *toks, *cots)


def late_kernel(steps, matrix_ref, weight_ref, *refs):
    toks, cots, scales = refs[0:2], refs[2:4], refs[4:8]
    early = refs[8:10]
    deltas_out, hidden_out, route_out = refs[10:13]
    accs = refs[13:15]
    step = pl.program_id(0)

    @pl.when(step == 0)
    def _():
        for acc in accs:
            acc[...] = jnp.zeros_like(acc)

    tok, cot = (
        jnp.concatenate([r[0][EARLY - 2 * BLOCK :], r[1][...]], axis=0) for r in (toks, cots)
    )
    accs[0][...] += product(two(weight_ref), tok, LAST)
    accs[1][...] += product(weight_ref[2], cot, LAST)

    @pl.when(step == steps - 1)
    def _():
        matrix = matrix_ref[...]
        both, back = (
            jnp.concatenate([first[...], acc[...]], axis=1) for first, acc in zip(early, accs)
        )
        units = back.shape[0]
        gate_pre, up_pre = both[:units], both[units:]
        lane = lax.broadcasted_iota(jnp.int32, (8, EXTRA), 1)
        first_lane = jnp.where(lane == 0, 1.0, 0.0).astype(jnp.bfloat16)
        scale = jnp.concatenate([ref[...] for ref in scales], axis=0)
        scale = product(first_lane, scale, LAST)[:1]
        grad = scale * back
        high = grad.astype(jnp.bfloat16)
        low = (grad - high.astype(jnp.float32)).astype(jnp.bfloat16)
        logistic = 1.0 / (1.0 + jnp.exp(-gate_pre))
        gated = gate_pre * logistic
        hidden = (gated * up_pre).astype(jnp.bfloat16)
        turned = product(jnp.concatenate([high, low, hidden], axis=0), matrix)
        grad = turned[:units] + turned[units : 2 * units]
        hidden = turned[2 * units :]
        hidden_out[...] = hidden.astype(jnp.bfloat16)
        deltas_out[:units] = (
            grad * up_pre * logistic * (1.0 + gate_pre * (1.0 - logistic))
        ).astype(jnp.bfloat16)
        deltas_out[units:] = (grad * gated).astype(jnp.bfloat16)
        route = jnp.sum(hidden * back, axis=0, keepdims=True).astype(jnp.bfloat16)
        route_out[...] = product(matrix, jnp.broadcast_to(route, (EXTRA, ROWS)), LAST).astype(
            jnp.bfloat16
        )


def forward_late(matrix, weights, toks, cots, early):
    units, width = weights.shape[1:]
    tile = 512
    steps = width // tile
    rows = pl.BlockSpec((BLOCK, tile), lambda i: (0, i))
    extra = pl.BlockSpec((BLOCK, EXTRA), lambda i: (0, width // EXTRA))
    shapes = [(2 * units, ROWS), (units, ROWS), (ROWS, EXTRA)]
    late = ROWS - EARLY
    return pl.pallas_call(
        functools.partial(late_kernel, steps),
        grid=(steps,),
        in_specs=[
            pl.BlockSpec((ROWS, ROWS), lambda i: (0, 0)),
            pl.BlockSpec((3, units, tile), lambda i: (0, 0, i)),
        ]
        + [rows] * 4
        + [extra] * 4
        + [pl.BlockSpec(array.shape, lambda i: (0, 0)) for array in early],
        out_specs=[pl.BlockSpec(shape, lambda i: (0, 0)) for shape in shapes],
        out_shape=[jax.ShapeDtypeStruct(shape, jnp.bfloat16) for shape in shapes],
        scratch_shapes=[pltpu.VMEM((n * units, late), jnp.float32) for n in (2, 1)],
        compiler_params=params("late"),
        cost_estimate=cost(6 * late * units * width, 6 * units * width + 12 * EARLY * units),
        name="forward_late",
    )(matrix, weights, *toks[2:], *cots[2:], *cots, *early)


def terms_kernel(deltas_ref, hidden_ref, *refs):
    toks, cots, scales, out_ref = refs[0:4], refs[4:8], refs[8:12], refs[12]
    tok = jnp.concatenate([ref[...] for ref in toks], axis=0)
    scaled = jnp.concatenate(
        [
            (ref[...].astype(jnp.float32) * scale[:, :1].astype(jnp.float32)).astype(jnp.bfloat16)
            for ref, scale in zip(cots, scales)
        ],
        axis=0,
    )
    share = out_ref.shape[2]
    units = hidden_ref.shape[0]
    kind = 0
    for left, right in ((deltas_ref, tok), (hidden_ref, scaled)):
        term = product(left[...], right)
        for first in range(0, left.shape[0], units):
            for owner in range(units // share):
                rows = term[first + owner * share : first + (owner + 1) * share]
                out_ref[owner, kind] = rows.astype(jnp.bfloat16)
            kind += 1


def terms(deltas, hidden, toks, cots, owners):
    units = hidden.shape[0]
    width = toks[0].shape[1]
    tile = 512
    rows = pl.BlockSpec((BLOCK, tile), lambda i: (0, i))
    extra = pl.BlockSpec((BLOCK, EXTRA), lambda i: (0, width // EXTRA))
    share = units // owners
    return pl.pallas_call(
        terms_kernel,
        grid=(width // tile,),
        in_specs=[pl.BlockSpec(array.shape, lambda i: (0, 0)) for array in (deltas, hidden)]
        + [rows] * 8
        + [extra] * 4,
        out_specs=pl.BlockSpec((owners, 3, share, tile), lambda i: (0, 0, 0, i)),
        out_shape=pltpu.HBM((owners, 3, share, width), jnp.bfloat16),
        compiler_params=params("terms"),
        cost_estimate=cost(6 * ROWS * units * width, 6 * units * width + 4 * ROWS * width),
        name="terms",
    )(deltas, hidden, *toks, *cots, *cots)


def inputs_kernel(tile, turn_ref, deltas_ref, weight_ref, route_ref, *refs):
    outs, delta_rows = refs[:SIDE], refs[SIDE]
    step = pl.program_id(0)

    @pl.when(step == 0)
    def _():
        delta_rows[...] = product(turn_ref[...], deltas_ref[...], LAST).astype(jnp.bfloat16)
        for p in range(SIDE):
            width = outs[p].shape[1]
            if width % tile:
                outs[p][:, width - EXTRA :] = route_ref[p * BLOCK : (p + 1) * BLOCK]

    value = product(delta_rows[...], two(weight_ref)).astype(jnp.bfloat16)
    columns = pl.ds(pl.multiple_of(step * tile, tile), tile)
    for p in range(SIDE):
        outs[p][:, columns] = value[p * BLOCK : (p + 1) * BLOCK]


def inputs(turn, deltas, weights, route, first, count, extra):
    units = weights.shape[1]
    tile = 512
    block = (BLOCK, count + extra)
    return pl.pallas_call(
        functools.partial(inputs_kernel, tile),
        grid=(count // tile,),
        in_specs=[
            pl.BlockSpec((ROWS, ROWS), lambda i: (0, 0)),
            pl.BlockSpec((2 * units, ROWS), lambda i: (0, 0)),
            pl.BlockSpec((2, units, tile), lambda i: (0, 0, first // tile + i)),
            pl.BlockSpec((ROWS, EXTRA), lambda i: (0, 0)),
        ],
        out_specs=[pl.BlockSpec(block, lambda i: (0, 0))] * SIDE,
        out_shape=[jax.ShapeDtypeStruct(block, jnp.bfloat16)] * SIDE,
        scratch_shapes=[pltpu.VMEM((ROWS, 2 * units), jnp.bfloat16)],
        compiler_params=params("inputs"),
        cost_estimate=cost(4 * ROWS * units * count, 4 * units * count + 2 * ROWS * count),
        name="inputs",
    )(turn, deltas, weights, route)


def shards(tokens, cotangent, expert_ids, route_weights, expert_weights):
    me = lax.axis_index("expert")
    z, x = me // SIDE, me % SIDE
    tok_rows, width = tokens.shape
    half = width // 2
    experts = SIDE * SIDE
    owners = lax.axis_size("dp")

    ids = expert_ids.T
    column = lax.broadcasted_iota(jnp.int32, (experts, 1, 1), 0)
    named = ids[None] == column
    routed = jnp.any(named, axis=1)
    earlier = (
        lax.broadcasted_iota(jnp.int32, (tok_rows, tok_rows), 0)
        < lax.broadcasted_iota(jnp.int32, (tok_rows, tok_rows), 1)
    ).astype(jnp.bfloat16)
    slots = jnp.dot(routed.astype(jnp.bfloat16), earlier, preferred_element_type=jnp.float32)
    slots = slots.astype(jnp.int32)
    expert = lax.broadcasted_iota(jnp.int32, (experts, 1), 0)
    far_z, far_x = (expert // SIDE - z) % SIDE, (expert % SIDE - x) % SIDE
    near_z = jnp.where(far_z >= 2, 5 - far_z, far_z)
    near_x = jnp.where(far_x >= 2, 5 - far_x, far_x)
    live = jnp.any(named, axis=0)

    def codes(block, lane):
        row = place(block, lane, slots)
        return jnp.where(live, jnp.sum(jnp.where(named, row[:, None, :], 0), axis=0), -1)

    def one_hot(code, first, count):
        row = lax.broadcasted_iota(jnp.int32, (count, tok_rows), 0) + first
        hot = row == code[0][None, :]
        for k in range(1, code.shape[0]):
            hot = hot | (row == code[k][None, :])
        return hot.astype(jnp.bfloat16)

    z_first = codes(near_z, near_x)
    x_first = codes(near_x, near_z)

    def row_scales(code, first):
        row = lax.broadcasted_iota(jnp.int32, (BLOCK, 1, 1), 0) + first
        scale = jnp.where(row == code[None], route_weights.T[None], 0.0)
        return jnp.sum(scale, axis=(1, 2))[:, None].astype(jnp.bfloat16)

    def pick(left, right):
        return jnp.dot(left, right, preferred_element_type=jnp.float32).astype(jnp.bfloat16)

    tok_blocks, cot_blocks = [], []
    for p in range(SIDE):
        tok_blocks.append(pick(one_hot(z_first, p * BLOCK, BLOCK), tokens))
        picked = pick(one_hot(x_first, p * BLOCK, BLOCK), cotangent)
        scale = jnp.broadcast_to(row_scales(x_first, p * BLOCK), (BLOCK, EXTRA))
        cot_blocks.append(jnp.concatenate([picked, scale], axis=1))

    turn = swap_matrix(False)
    small_turn = swap_matrix(True)
    same = (jnp.arange(ROWS)[:, None] == jnp.arange(ROWS)[None, :]).astype(jnp.bfloat16)

    def near_then_far(blocks, axis):
        near = [blocks[0]] + [move(blocks[p], axis, HOPS[p]) for p in (1, 2)]
        far = lax.optimization_barrier((blocks[3], near[1], near[2]))
        return [near[0], far[1], far[2], move(far[0], axis, HOPS[3])]

    toks = near_then_far(swap_blocks(small_turn, near_then_far(tok_blocks, "z")), "x")
    cots = near_then_far(swap_blocks(small_turn, near_then_far(cot_blocks, "x")), "z")

    weights = expert_weights[0].transpose(1, 0, 2)
    early = forward_early(weights, toks[:3], cots[:3])
    deltas, hidden, route = forward_late(turn, weights, toks, cots, early)
    partial_sums = terms(deltas, hidden, toks, cots, owners)
    summed = lax.psum_scatter(partial_sums, "dp", scatter_dimension=0, tiled=True)
    weight_grad = summed.astype(jnp.float32).transpose(0, 2, 1, 3)

    right = inputs(turn, deltas, weights, route, half, half, 0)
    left = inputs(same, deltas, weights, route, 0, half, EXTRA)
    left = spread(swap_blocks(small_turn, spread(left, "x", -1)), "z", -1)
    right = spread(swap_blocks(small_turn, spread(right, "z", -1)), "x", -1)

    def combine(blocks, code):
        return jnp.einsum(
            "ct,cd->td",
            one_hot(code, 0, ROWS),
            jnp.concatenate(blocks, axis=0),
            preferred_element_type=jnp.float32,
        ).astype(jnp.bfloat16)

    input_grad = jnp.concatenate(
        [combine([b[:, :half] for b in left], z_first), combine(right, x_first)], axis=1
    )
    route_mine = jnp.concatenate([b[:, half] for b in left], axis=0).astype(jnp.float32)
    row = lax.broadcasted_iota(jnp.int32, (ROWS, 1, 1), 0)
    route_grad = jnp.sum(jnp.where(row == z_first[None], route_mine[:, None, None], 0.0), axis=0)
    return input_grad, route_grad.astype(jnp.bfloat16).T, weight_grad


def solution(mesh):
    rows = P(("dp", "expert"), None)
    return jax.shard_map(
        shards,
        mesh=mesh,
        in_specs=(rows, rows, rows, rows, P("expert", None, None, None)),
        out_specs=(rows, rows, P("expert", "dp", None, None)),
        check_vma=False,
    )
```
